32 devices in a mesh: group: 2 (over y), seq: 4 (over z), member: 4 (over x, core).
Axes of the slice: x: 2, y: 2, z: 4, core: 2. Of those that a mesh axis runs over, the one named last changes fastest.
Arguments:
- tokens: bfloat16 [8, 2048, 1024], P(('group', 'member'), 'seq'), parts along dimension 0, may hold values from -6 to 6
- input_weight: bfloat16 [1024, 3072], replicated, may hold values from -0.1875 to 0.1875
- output_weight: bfloat16 [1024, 1024], replicated, may hold values from -0.75 to 0.75
- decoder_weight: bfloat16 [1024, 128], replicated, may hold values from -0.1875 to 0.1875
- neighbours: int32 [4096, 4], P('seq'), may hold values from 0 to 2047, as said below
- observed: float32 [8192, 128], P(('group', 'seq')), parts along dimension 0, may hold values from -6 to 6
- cell_area: float32 [4096], P('seq'), may hold values from 0.3 to 3
Outputs:
- attention_cotangent: bfloat16 [8, 2048, 1024], P(('group', 'member'), 'seq'), parts along dimension 0
- output_gradient: float32 [2048, 1024], P(('group', 'seq')), parts along dimension 0
- decoder_gradient: float32 [2048, 128], P('group'), parts along dimension 0
The draws below stay inside these ranges and needn't reach their ends.
There are 2 independent parts, one for each index of `group`. The reference program is written for one: setup_inputs(seed, part) draws one part's arguments, and reference() takes and returns one part's arrays. A program takes and returns all parts, laid end to end along the dimension named above; an argument that names none is the same for every part. Nothing has to cross between parts.
Inputs may be any that keep to these rules, and one draw needn't show every extreme that they name: `neighbours`: the grid points held by index s of seq (rows s * 1024 to (s + 1) * 1024 - 1) name only tokens from s * 512 - 128 to (s + 1) * 512 + 127, cut to the tokens that exist; both ends of that range are named in every such block.
All inputs are finite; a program needn't handle non-finite values.
Results may differ from the reference program's by a relative error of at most 0.014.
Values may be sent and summed in bfloat16 or wider, within the bound.
A program may use at most 128 MiB of HBM per device.

```python
import math
import jax
import jax.numpy as jnp
from jax import lax

HEAD_DIM = 64
D = 1024
F = 128
WINDOW = 512
K = 4
REACH = 128
TOK_DEV = 512
GRID_DEV = 1024
TOKENS = 2048
GRID = 4096
MEMBERS = 4


def draw_neighbours(key, part):
    rows = jnp.arange(GRID, dtype=jnp.int32)
    owner = rows // GRID_DEV
    local_row = rows % GRID_DEV
    span = TOK_DEV + 2 * REACH
    offsets = jax.random.randint(key, (GRID, K), 0, span, dtype=jnp.int32)
    column = jnp.arange(K, dtype=jnp.int32)
    offsets = jnp.where((local_row[:, None] == 0) & (column[None, :] == 0), 0, offsets)
    offsets = jnp.where((local_row[:, None] == GRID_DEV - 1) & (column[None, :] == K - 1), span - 1, offsets)
    chosen = owner[:, None] * TOK_DEV - REACH + offsets
    return jnp.clip(chosen, 0, TOKENS - 1).astype(jnp.int32)


def levels(own_key, dims, cuts, least, top_value):
    level, own = 1.0, jax.random.fold_in(own_key, 6)
    for dim, parts in cuts:
        steps = jnp.exp(jax.random.uniform(jax.random.fold_in(own, dim), (parts,), jnp.float32, least / len(cuts), top_value / len(cuts)))
        level = level * jnp.repeat(steps, dims[dim] // parts).reshape([-1 if axis == dim else 1 for axis in range(len(dims))])
    return level


def normal_values(own_key, extent, scale, most, pieces=(), kind=jnp.bfloat16):
    gain = levels(own_key, extent, pieces, -0.22, 0.18) if pieces else 1.0
    array = jax.random.normal(own_key, extent, jnp.float32) * scale * gain
    return jnp.minimum(jnp.maximum(array, -most), most).astype(kind)


def setup_inputs(seed: int = 0, part: int = 0) -> dict:
    key_list = jax.random.split(jax.random.key(seed), 8)
    part_keys = jax.random.split(jax.random.fold_in(key_list[7], part), 8)
    return {
        "tokens": normal_values(part_keys[0], (MEMBERS, TOKENS, D), 1.0, 6.0, ((0, 4), (1, 4))),
        "input_weight": normal_values(key_list[1], (D, 3 * D), D ** -0.5, 0.1875),
        "output_weight": normal_values(key_list[2], (D, D), HEAD_DIM ** -0.5, 0.75),
        "decoder_weight": normal_values(key_list[3], (D, F), D ** -0.5, 0.1875),
        "neighbours": draw_neighbours(jax.random.fold_in(key_list[7], 71), part),
        "observed": normal_values(part_keys[5], (GRID, F), 1.0, 6.0, ((0, 4),), jnp.float32),
        "cell_area": jnp.clip(jnp.exp(math.log(3.0) - 2.3025851 * jax.random.uniform(key_list[6], (GRID,), jnp.float32) ** levels(key_list[6], (GRID,), ((0, 4),), -0.2, 0.2)), 0.3, 3.0),
    }


smooth = 0.1

def normalize(rows):
    values = rows.astype(jnp.float32)
    centre = lax.optimization_barrier(jnp.mean(values, axis=-1, keepdims=True))
    spread = lax.optimization_barrier(jnp.mean((values - centre) ** 2, axis=-1, keepdims=True))
    return ((values - centre) * lax.rsqrt(spread + 1e-05)).astype(jnp.bfloat16)

def head_norm(part):
    return (part * lax.rsqrt(lax.optimization_barrier(jnp.mean(part * part, axis=-1, keepdims=True)) + 1e-06)).astype(jnp.bfloat16)

def project(own_tokens, input_weight):
    length, width = own_tokens.shape
    heads = width // HEAD_DIM
    mixed = jnp.dot(normalize(own_tokens), input_weight, preferred_element_type=jnp.float32)
    query = head_norm(mixed[:, :width].reshape(length, heads, HEAD_DIM))
    keys = head_norm(mixed[:, width:2 * width].reshape(length, heads, HEAD_DIM))
    values = mixed[:, 2 * width:].reshape(length, heads, HEAD_DIM).astype(jnp.bfloat16)
    return (query, keys, values)

def attend(query, keys, values, key_base, total):
    length, heads, depth = query.shape
    half = (keys.shape[0] - length) // 2
    block = min(length, max(8, 512 // heads))
    count = length // block
    scale = depth ** (-0.5)

    def one_block(index):
        start = index * block
        query_block = lax.dynamic_slice_in_dim(query, start, block, 0).astype(jnp.float32)
        key_block = lax.dynamic_slice_in_dim(keys, start, block + 2 * half, 0).astype(jnp.float32)
        value_block = lax.dynamic_slice_in_dim(values, start, block + 2 * half, 0).astype(jnp.float32)
        scores = jnp.einsum('qhe,khe->hqk', query_block, key_block) * scale
        query_place = jnp.arange(block, dtype=jnp.int32)[:, None]
        key_place = jnp.arange(block + 2 * half, dtype=jnp.int32)[None, :]
        relative = key_place - query_place
        position = key_base + start + key_place
        valid = (relative >= 0) & (relative < 2 * half) & (position >= 0) & (position < total)
        weights = jnp.where(valid[None], jnp.exp(scores), 0.0)
        shares = (weights / lax.optimization_barrier(jnp.sum(weights, axis=-1, keepdims=True))).astype(jnp.bfloat16)
        return jnp.einsum('hqk,khe->qhe', shares.astype(jnp.float32), value_block).astype(jnp.bfloat16)
    result = lax.map(one_block, jnp.arange(count, dtype=jnp.int32))
    return result.reshape(length, heads, depth)

def slope(diff):
    return diff * lax.rsqrt(diff * diff + smooth * smooth)

def ensemble_cotangent(own, every, observed, cell_area):
    members = every.shape[0]
    pairs = lax.optimization_barrier(jnp.sum(slope(own[..., None, :, :] - every), axis=-3))
    single = slope(own - observed)
    return (cell_area[:, None] * (single / members - pairs / (members * (members - 1)))).astype(jnp.bfloat16)

def reference(tokens, input_weight, output_weight, decoder_weight, neighbours, observed, cell_area):
    members, total, width = tokens.shape
    half = WINDOW // 2
    fan_count = neighbours.shape[1]

    def forward(own_tokens):
        query, keys, values = project(own_tokens, input_weight)
        padding = jnp.zeros((half,) + keys.shape[1:], jnp.bfloat16)
        keys = jnp.concatenate([padding, keys, padding], axis=0)
        values = jnp.concatenate([padding, values, padding], axis=0)
        attended = attend(query, keys, values, -half, total).reshape(total, width)
        latent = (own_tokens.astype(jnp.float32) + jnp.dot(attended, output_weight, preferred_element_type=jnp.float32)).astype(jnp.bfloat16)
        pooled = (lax.optimization_barrier(jnp.sum(latent[neighbours].astype(jnp.float32), axis=1)) / fan_count).astype(jnp.bfloat16)
        fields = jnp.dot(pooled, decoder_weight, preferred_element_type=jnp.float32)
        return (attended, pooled, fields)
    attended, pooled, fields = lax.map(forward, tokens)

    def backward(carry, inputs):
        output_total, decoder_total = carry
        attended_one, pooled_one, fields_one = inputs
        field_cotangent = ensemble_cotangent(fields_one, fields, observed, cell_area)
        decoder_total = decoder_total + jnp.dot(pooled_one.T, field_cotangent, preferred_element_type=jnp.float32)
        pooled_cotangent = jnp.dot(field_cotangent, decoder_weight.T, preferred_element_type=jnp.float32)
        share = pooled_cotangent / fan_count
        latent_cotangent = jnp.zeros((total, width), jnp.float32)
        for column in range(fan_count):
            latent_cotangent = latent_cotangent.at[neighbours[:, column]].add(share)
        latent_cotangent = latent_cotangent.astype(jnp.bfloat16)
        output_total = output_total + jnp.dot(attended_one.T, latent_cotangent, preferred_element_type=jnp.float32)
        cotangent = jnp.dot(latent_cotangent, output_weight.T, preferred_element_type=jnp.float32).astype(jnp.bfloat16)
        return ((output_total, decoder_total), cotangent)
    start_carry = (jnp.zeros((width, width), jnp.float32), jnp.zeros((width, decoder_weight.shape[1]), jnp.float32))
    (output_total, decoder_total), attention_cotangent = lax.scan(backward, start_carry, (attended, pooled, fields))
    output_gradient = output_total / math.sqrt(members * total)
    decoder_gradient = decoder_total / math.sqrt(members * observed.shape[0])
    return (attention_cotangent, output_gradient, decoder_gradient)
```

```python
import functools
import math

import jax
import jax.numpy as jnp
from jax import lax
from jax.experimental import pallas as pl
from jax.experimental.pallas import tpu as pltpu
from jax.sharding import PartitionSpec as P

HEAD_DIM = 64
WINDOW = 512
REACH = 128
LANES = 128
COLS = 512

smooth = 0.1
f32 = jnp.float32
bf16 = jnp.bfloat16


def normalize(rows):
    values = rows.astype(f32)
    centre = jnp.mean(values, axis=-1, keepdims=True)
    values = values - centre
    spread = jnp.mean(values * values, axis=-1, keepdims=True)
    return (values * lax.rsqrt(spread + 1e-05)).astype(bf16)


def place_columns(mixed, scale):
    side = 256
    down = lax.broadcasted_iota(jnp.int32, (side, side), 0) >> 6
    across = lax.broadcasted_iota(jnp.int32, (side, side), 1) >> 6
    same = jnp.where(down == across, 1.0 / HEAD_DIM, 0.0).astype(bf16)
    pieces = []
    for at in range(0, mixed.shape[1], side):
        piece = mixed[:, at : at + side]
        mean = jnp.dot((piece * piece).astype(bf16), same, preferred_element_type=f32)
        pieces.append((piece * (lax.rsqrt(mean + 1e-06) * scale)).astype(bf16))
    return jnp.concatenate(pieces, axis=1)


def project(normed, weight, out, first, waits):
    width = weight.shape[0]
    for at in range(first, weight.shape[1], COLS):
        if waits:
            waits[at // COLS].wait()
        mixed = jnp.dot(normed[...], weight[:, at : at + COLS], preferred_element_type=f32)
        if at < 2 * width:
            mixed = place_columns(mixed, HEAD_DIM**-0.5 if at < width else 1.0)
        out[:, at - first : at - first + COLS] = mixed.astype(bf16)


def lane_block(j):
    return pl.ds(pl.multiple_of(j * LANES, LANES), LANES)


def low_lanes():
    return lax.broadcasted_iota(jnp.int32, (1, LANES), 1) < HEAD_DIM


def one_head(pair, head):
    return jnp.where(low_lanes() == (head == 0), pair, jnp.zeros_like(pair))


def with_counts(pair, head, real):
    ones = jnp.full(pair.shape, real, f32).astype(bf16)
    first = low_lanes()
    return jnp.where(first, pair, ones) if head == 0 else jnp.where(first, ones, pair)


def score(query, keys):
    return lax.dot_general(query, keys, (((1,), (1,)), ((), ())), preferred_element_type=f32)


def window_corner(scores, upper):
    rows = scores.shape[0] // 2
    down = lax.broadcasted_iota(jnp.int32, (rows, rows), 0)
    across = lax.broadcasted_iota(jnp.int32, (rows, rows), 1)
    late = across >= down
    blank = jnp.zeros((rows, rows), bf16)

    def corner(piece):
        weights = jnp.exp(piece)
        return (jnp.where(late, weights, 0.0) if upper else jnp.where(late, 0.0, weights)).astype(bf16)

    ends = (corner(scores[:rows, :rows]), corner(scores[rows:, rows:]))
    if upper:
        rest = jnp.exp(scores[:rows, rows:]).astype(bf16)
        lines = [[ends[0], rest], [blank, ends[1]]]
    else:
        rest = jnp.exp(scores[rows:, :rows]).astype(bf16)
        lines = [[ends[0], blank], [rest, ends[1]]]
    return jnp.concatenate([jnp.concatenate(line, axis=1) for line in lines], axis=0)


def attend_own(j, own, partial):
    rows, width = own.shape[0], own.shape[1] // 3
    half = rows // 2
    query = own[:, lane_block(j)]
    keys = own[:, lane_block(j + width // LANES)]
    values = own[:, lane_block(j + 2 * (width // LANES))]
    for head in range(2):
        scores = score(one_head(query, head), keys)
        early = [
            jnp.exp(scores[:half, :half]).astype(bf16), window_corner(scores[:half, half:], False),
        ]
        later = [
            window_corner(scores[half:, :half], True), jnp.exp(scores[half:, half:]).astype(bf16),
        ]
        weights = jnp.concatenate(
            [jnp.concatenate(early, axis=1), jnp.concatenate(later, axis=1)], axis=0
        )
        partial[2 * j + head] = jnp.dot(
            weights, with_counts(values, head, 1.0), preferred_element_type=f32
        )


def attend_beside(j, index, own, side, partial, attended, there):
    width = attended.shape[1]
    half = own.shape[0] // 2
    rows = slice(index * half, (index + 1) * half)
    query = own[rows, lane_block(j)]
    keys = side[rows, lane_block(j)]
    values = side[rows, lane_block(j + width // LANES)]
    totals = []
    for head in range(2):
        weights = window_corner(score(one_head(query, head), keys), index == 0)
        totals.append(
            jnp.dot(weights, with_counts(values, head, there), preferred_element_type=f32)
            + partial[2 * j + head, rows, :]
        )
    first = low_lanes()
    above = jnp.where(first, totals[0], totals[1])
    below = jnp.where(
        first, pltpu.roll(totals[0], HEAD_DIM, 1), pltpu.roll(totals[1], HEAD_DIM, 1)
    )
    attended[rows, lane_block(j)] = (above / below).astype(bf16)


def slope(diff):
    return diff * lax.rsqrt(diff * diff + smooth * smooth)


def copy_to(source, target, send, arrive, seq, member):
    return pltpu.make_async_remote_copy(
        src_ref=source,
        dst_ref=target,
        send_sem=send,
        recv_sem=arrive,
        device_id={"seq": seq, "member": member},
        device_id_type=pl.DeviceIdType.MESH,
    )


def layer_kernel(
    seqs, members, decoder, neighbours, area, tokens_far, weight_far, observed_far, output_far,
    middle_out, rows_out, decoder_out, joint,
    every, counts, turned, middle, edges, edges_in, terms, terms_in, sums, sums_in, mine,
    gathered_rows, gathered, tokens, attended, observed, output_weight,
    weight, normed, beside, own_parts, side_parts, mapped, partial, seen,
    halo_send, halo_in,
    local_sem, field_send, field_in, side_send, side_in, edge_send, edge_in, term_send, term_in,
    sum_send, sum_in, row_send, row_in, all_send, all_in,
):
    s, m = lax.axis_index("seq"), lax.axis_index("member")
    peers = seqs * members
    me = s * members + m
    tok_rows, fields = mapped.shape
    fan, grid_rows = neighbours.shape
    wide = tok_rows + 2 * REACH
    width = tokens.shape[1]
    chunk = width // peers

    def peer(step):
        flat = lax.rem(me + step, peers)
        return flat // members, lax.rem(flat, members)

    barrier = pltpu.get_barrier_semaphore()

    @pl.loop(1, peers)
    def _(step):
        seq, member = peer(step)
        pl.semaphore_signal(
            barrier, inc=1, device_id={"seq": seq, "member": member},
            device_id_type=pl.DeviceIdType.MESH,
        )

    columns = weight.shape[1] // COLS
    loads = [
        pltpu.make_async_copy(far, near, local_sem.at[i])
        for i, (far, near) in enumerate(
            [(tokens_far, tokens)]
            + [
                (weight_far.at[:, pl.ds(i * COLS, COLS)], weight.at[:, pl.ds(i * COLS, COLS)])
                for i in range(columns)
            ]
            + [(output_far, output_weight), (observed_far, observed)]
        )
    ]
    for load in loads:
        load.start()
    has_left, has_right = s > 0, s < seqs - 1
    half = WINDOW // 2

    def halo_copy(to_right):
        start, land, seq = (tok_rows - half, 0, s + 1) if to_right else (0, half, s - 1)
        return copy_to(
            tokens_far.at[pl.ds(start, half), :], beside.at[pl.ds(land, half), :],
            halo_send.at[to_right], halo_in.at[to_right], seq, m,
        )

    @pl.when(jnp.logical_not(has_left))
    def _():
        beside[:half, :] = jnp.zeros((half, width), bf16)

    @pl.when(jnp.logical_not(has_right))
    def _():
        beside[half:, :] = jnp.zeros((half, width), bf16)

    pl.semaphore_wait(barrier, peers - 1)

    @pl.when(has_right)
    def _():
        halo_copy(1).start()

    @pl.when(has_left)
    def _():
        halo_copy(0).start()

    loads[0].wait()
    normed[...] = normalize(tokens[...])
    project(normed, weight, own_parts, 0, loads[1 : 1 + columns])
    loads[1 + columns].wait()
    joint[...] = jnp.dot(
        output_weight[...], decoder[...], preferred_element_type=f32
    ).astype(bf16)
    mapped[...] = jnp.dot(tokens[...], decoder[...], preferred_element_type=f32)
    base = s * tok_rows - REACH
    block = 128
    loads[2 + columns].wait()

    @pl.loop(0, grid_rows // block)
    def _(i):
        cells = pl.ds(pl.multiple_of(i * block, block), block)
        local = neighbours[:, cells] - base
        place = lax.broadcasted_iota(jnp.int32, (wide, block), 0)
        total = jnp.zeros((wide, block), f32)
        for k in range(fan):
            total += jnp.where(local[k : k + 1, :] == place, 1.0 / fan, 0.0)
        counts[:, cells] = total.astype(bf16)
        seen[:, cells] = observed[cells, :].T

    blocks = width // LANES
    group = math.gcd(blocks, 4)

    @pl.loop(0, blocks // group)
    def _(i):
        for k in range(group):
            attend_own(i * group + k, own_parts, partial)

    @pl.when(has_left)
    def _():
        halo_copy(0).wait_send()
        halo_copy(1).wait_recv()

    @pl.when(has_right)
    def _():
        halo_copy(1).wait_send()
        halo_copy(0).wait_recv()

    normed[...] = normalize(beside[...])
    project(normed, weight, side_parts, width, None)
    def field_copy(index, step):
        cells = pl.ds(REACH + index * half, half)
        return copy_to(
            every.at[pl.ds(0, fields), cells], every.at[pl.ds(step * fields, fields), cells],
            field_send.at[index, step], field_in.at[index, step], s, lax.rem(m + step, members),
        )

    def side_copy(side, step):
        start, land, seq = ((tok_rows, 0, s + 1), (REACH, REACH + tok_rows, s - 1))[side]
        return copy_to(
            every.at[pl.ds(0, fields), pl.ds(start, REACH)],
            every.at[pl.ds(step * fields, fields), pl.ds(land, REACH)],
            side_send.at[side, step], side_in.at[side, step], seq, lax.rem(m + step, members),
        )

    for index in range(2):
        there = jnp.where((has_left, has_right)[index], 1.0, 0.0).astype(f32)
        for j in range(blocks):
            attend_beside(j, index, own_parts, side_parts, partial, attended, there)
        at = index * half
        total = mapped[at : at + half, :] + jnp.dot(
            attended[at : at + half, :], joint[...], preferred_element_type=f32
        )
        every[:fields, REACH + at : REACH + at + half] = total.T.astype(bf16)
        for step in range(1, members):
            field_copy(index, step).start()

        @pl.when((has_left, has_right)[index])
        def _():
            for step in range(members):
                side_copy(1 - index, step).start()

    @pl.when(jnp.logical_not(has_left))
    def _():
        every[:, :REACH] = jnp.zeros((members * fields, REACH), bf16)
        edges_in[0] = jnp.zeros((fields, REACH), bf16)

    @pl.when(jnp.logical_not(has_right))
    def _():
        every[:, wide - REACH :] = jnp.zeros((members * fields, REACH), bf16)
        edges_in[1] = jnp.zeros((fields, REACH), bf16)

    for index in range(2):
        for step in range(1, members):
            field_copy(index, step).wait()

    @pl.when(has_left)
    def _():
        for step in range(members):
            side_copy(1, step).wait_send()
            side_copy(0, step).wait_recv()

    @pl.when(has_right)
    def _():
        for step in range(members):
            side_copy(0, step).wait_send()
            side_copy(1, step).wait_recv()

    block = 256

    @pl.loop(0, grid_rows // block)
    def _(i):
        cells = pl.ds(pl.multiple_of(i * block, block), block)
        found = jnp.dot(every[...], counts[:, cells], preferred_element_type=f32)
        mean = found[:fields, :]
        pairs = jnp.zeros((fields, block), f32)
        for step in range(members):
            pairs += slope(mean - found[step * fields : (step + 1) * fields, :])
        single = slope(mean - seen[:, cells])
        turned[:, cells] = (
            area[:, cells]
            * (single * (1.0 / members) - pairs * (1.0 / (members * (members - 1))))
        ).astype(bf16)

    def spread(start, size):
        return lax.dot_general(
            turned[...], counts[start : start + size, :], (((1,), (1,)), ((), ())),
            preferred_element_type=f32,
        )

    edges[0] = spread(0, REACH).astype(bf16)
    edges[1] = spread(REACH + tok_rows, REACH).astype(bf16)

    def edge_copy(side):
        return copy_to(
            edges.at[side], edges_in.at[1 - side], edge_send.at[side], edge_in.at[side],
            s - 1 if side == 0 else s + 1, m,
        )

    @pl.when(has_left)
    def _():
        edge_copy(0).start()

    @pl.when(has_right)
    def _():
        edge_copy(1).start()

    middle[...] = spread(REACH, tok_rows)
    inner = middle[:, REACH : tok_rows - REACH].astype(bf16)
    output_term = jnp.dot(
        inner, attended[REACH : tok_rows - REACH, :], preferred_element_type=f32
    )

    @pl.when(has_left)
    def _():
        edge_copy(0).wait_send()
        edge_copy(1).wait_recv()

    @pl.when(has_right)
    def _():
        edge_copy(1).wait_send()
        edge_copy(0).wait_recv()

    middle[:, :REACH] += edges_in[0].astype(f32)
    middle[:, tok_rows - REACH :] += edges_in[1].astype(f32)
    whole = middle[...].astype(bf16)
    output_term += jnp.dot(whole[:, :REACH], attended[:REACH, :], preferred_element_type=f32)
    output_term += jnp.dot(
        whole[:, tok_rows - REACH :], attended[tok_rows - REACH :, :],
        preferred_element_type=f32,
    )

    def put(part, value):
        rows = value.T.astype(bf16)
        for member in range(members):
            for seq in range(seqs):
                at = (seq * members + member) * chunk
                terms[part, member, seq] = rows[at : at + chunk, :]

    def term_copy(part, step):
        member = lax.rem(m + step, members)
        return copy_to(
            terms.at[part, member], terms_in.at[part, step],
            term_send.at[part, step], term_in.at[part, step], s, member,
        )

    def sum_copy(part, step):
        seq = lax.rem(s + step, seqs)
        return copy_to(
            sums.at[part, seq], sums_in.at[part, step],
            sum_send.at[part, step], sum_in.at[part, step], seq, m,
        )

    put(0, output_term)
    for step in range(1, members):
        term_copy(0, step).start()
    decoder_term = jnp.dot(whole, tokens[...], preferred_element_type=f32)
    decoder_term += jnp.dot(
        output_term.astype(bf16), output_weight[...], preferred_element_type=f32
    )
    put(1, decoder_term)
    for step in range(1, members):
        term_copy(1, step).start()
    middle_out[...] = middle[...].T.astype(bf16)
    for part in range(2):
        for step in range(1, members):
            term_copy(part, step).wait()
        total = terms[part, m].astype(f32)
        for step in range(1, members):
            total += terms_in[part, step].astype(f32)
        sums[part] = total.astype(bf16)

        @pl.loop(1, seqs)
        def _(step):
            sum_copy(part, step).start()

    def row_copy(step):
        return copy_to(
            mine.at[0], gathered_rows.at[m], row_send.at[step], row_in.at[step],
            s, lax.rem(m + step, members),
        )

    def all_copy(step):
        seq, member = peer(step)
        return copy_to(
            mine.at[1], gathered.at[me], all_send.at[step], all_in.at[step], seq, member
        )

    for part in range(2):

        @pl.loop(1, seqs)
        def _(step):
            sum_copy(part, step).wait()

        total = sums[part, s].astype(f32)
        for step in range(1, seqs):
            total += sums_in[part, step].astype(f32)
        mine[part] = total.astype(bf16)
        if part == 0:
            for step in range(1, members):
                row_copy(step).start()
        else:

            @pl.loop(1, peers)
            def _(step):
                all_copy(step).start()

    gathered_rows[m] = mine[0]
    gathered[me] = mine[1]
    for step in range(1, members):
        row_copy(step).wait()
    rows_out[...] = gathered_rows[...]

    @pl.loop(1, peers)
    def _(step):
        all_copy(step).wait()

    decoder_out[...] = gathered[...]


def layer(decoder, neighbours, area, tokens, weight, observed, output_weight, seqs, members):
    tok_rows, width = tokens.shape
    fields = decoder.shape[1]
    grid_rows = neighbours.shape[1]
    wide = tok_rows + 2 * REACH
    peers = seqs * members
    chunk = width // peers
    near = pl.BlockSpec(memory_space=pltpu.VMEM)
    far = pl.BlockSpec(memory_space=pl.ANY)
    dma = pltpu.SemaphoreType.DMA
    return pl.pallas_call(
        functools.partial(layer_kernel, seqs, members),
        in_specs=[near] * 3 + [far] * 4,
        out_specs=[near] * 4,
        out_shape=[
            jax.ShapeDtypeStruct((tok_rows, fields), bf16),
            jax.ShapeDtypeStruct((members, chunk, fields), bf16),
            jax.ShapeDtypeStruct((peers, chunk, fields), bf16),
            jax.ShapeDtypeStruct((width, fields), bf16),
        ],
        scratch_shapes=[
            pltpu.VMEM((members * fields, wide), bf16),
            pltpu.VMEM((wide, grid_rows), bf16),
            pltpu.VMEM((fields, grid_rows), bf16),
            pltpu.VMEM((fields, tok_rows), f32),
            pltpu.VMEM((2, fields, REACH), bf16),
            pltpu.VMEM((2, fields, REACH), bf16),
            pltpu.VMEM((2, members, seqs, chunk, fields), bf16),
            pltpu.VMEM((2, members, seqs, chunk, fields), bf16),
            pltpu.VMEM((2, seqs, chunk, fields), bf16),
            pltpu.VMEM((2, seqs, chunk, fields), bf16),
            pltpu.VMEM((2, chunk, fields), bf16),
            pltpu.VMEM((members, chunk, fields), bf16),
            pltpu.VMEM((peers, chunk, fields), bf16),
            pltpu.VMEM(tokens.shape, bf16),
            pltpu.VMEM(tokens.shape, bf16),
            pltpu.VMEM(observed.shape, f32),
            pltpu.VMEM(output_weight.shape, bf16),
            pltpu.VMEM(weight.shape, bf16),
            pltpu.VMEM(tokens.shape, bf16),
            pltpu.VMEM((WINDOW, width), bf16),
            pltpu.VMEM((tok_rows, 3 * width), bf16),
            pltpu.VMEM((WINDOW, 2 * width), bf16),
            pltpu.VMEM((tok_rows, fields), f32),
            pltpu.VMEM((2 * (width // LANES), tok_rows, LANES), f32),
            pltpu.VMEM((fields, grid_rows), f32),
            dma((2,)),
            dma((2,)),
            dma((3 + weight.shape[1] // COLS,)),
            dma((2, members)),
            dma((2, members)),
            dma((2, members)),
            dma((2, members)),
            dma((2,)),
            dma((2,)),
            dma((2, members)),
            dma((2, members)),
            dma((2, seqs)),
            dma((2, seqs)),
            dma((members,)),
            dma((members,)),
            dma((peers,)),
            dma((peers,)),
        ],
        compiler_params=pltpu.CompilerParams(
            vmem_limit_bytes=56 << 20, collective_id=0, has_side_effects=True
        ),
    )(decoder, neighbours, area, tokens, weight, observed, output_weight)


def body(tokens, input_weight, output_weight, decoder_weight, neighbours, observed, cell_area):
    own_tokens = tokens[0]
    tok_rows, width = own_tokens.shape
    fields = decoder_weight.shape[1]
    seqs = lax.axis_size("seq")
    members = lax.axis_size("member")
    grid_rows = neighbours.shape[0]
    middle, rows, decoder_sum, joint = layer(
        decoder_weight, neighbours.T, cell_area[None, :], own_tokens, input_weight, observed,
        output_weight, seqs, members,
    )
    attention_cotangent = lax.dot_general(
        middle, joint, (((1,), (1,)), ((), ())), preferred_element_type=f32
    ).astype(bf16)
    output_gradient = lax.dot_general(
        rows.reshape(width // seqs, fields), decoder_weight, (((1,), (1,)), ((), ())),
        preferred_element_type=f32,
    ) * (1.0 / math.sqrt(members * tok_rows * seqs))
    decoder_gradient = decoder_sum.reshape(width, fields).astype(f32) * (
        1.0 / math.sqrt(members * grid_rows * seqs)
    )
    return (attention_cotangent[None], output_gradient, decoder_gradient)


def solution(mesh):
    in_specs = (
        P(("group", "member"), "seq", None),
        P(),
        P(),
        P(),
        P("seq", None),
        P(("group", "seq"), None),
        P("seq"),
    )
    out_specs = (P(("group", "member"), "seq", None), P(("group", "seq"), None), P("group", None))
    return jax.shard_map(body, mesh=mesh, in_specs=in_specs, out_specs=out_specs, check_vma=False)
```

```python
import functools
import math

import jax
import jax.numpy as jnp
from jax import lax
from jax.experimental import pallas as pl
from jax.experimental.pallas import tpu as pltpu
from jax.sharding import PartitionSpec as P

HEAD_DIM = 64
WINDOW = 512
REACH = 128
LANES = 128
COLS = 512

smooth = 0.1
f32 = jnp.float32
bf16 = jnp.bfloat16


def normalize(rows):
    values = rows.astype(f32)
    centre = jnp.mean(values, axis=-1, keepdims=True)
    values = values - centre
    spread = jnp.mean(values * values, axis=-1, keepdims=True)
    return (values * lax.rsqrt(spread + 1e-05)).astype(bf16)


def place_columns(mixed, scale):
    side = 256
    down = lax.broadcasted_iota(jnp.int32, (side, side), 0) >> 6
    across = lax.broadcasted_iota(jnp.int32, (side, side), 1) >> 6
    same = jnp.where(down == across, 1.0 / HEAD_DIM, 0.0).astype(bf16)
    pieces = []
    for at in range(0, mixed.shape[1], side):
        piece = mixed[:, at : at + side]
        mean = jnp.dot((piece * piece).astype(bf16), same, preferred_element_type=f32)
        pieces.append((piece * (lax.rsqrt(mean + 1e-06) * scale)).astype(bf16))
    return jnp.concatenate(pieces, axis=1)


def project(normed, weight, out, first, waits):
    width = weight.shape[0]
    for at in range(first, weight.shape[1], COLS):
        if waits:
            waits[at // COLS].wait()
        mixed = jnp.dot(normed[...], weight[:, at : at + COLS], preferred_element_type=f32)
        if at < 2 * width:
            mixed = place_columns(mixed, HEAD_DIM**-0.5 if at < width else 1.0)
        out[:, at - first : at - first + COLS] = mixed.astype(bf16)


def lane_block(j):
    return pl.ds(pl.multiple_of(j * LANES, LANES), LANES)


def low_lanes():
    return lax.broadcasted_iota(jnp.int32, (1, LANES), 1) < HEAD_DIM


def one_head(pair, head):
    return jnp.where(low_lanes() == (head == 0), pair, jnp.zeros_like(pair))


def with_counts(pair, head, real):
    ones = jnp.full(pair.shape, real, f32).astype(bf16)
    first = low_lanes()
    return jnp.where(first, pair, ones) if head == 0 else jnp.where(first, ones, pair)


def score(query, keys):
    return lax.dot_general(query, keys, (((1,), (1,)), ((), ())), preferred_element_type=f32)


def window_corner(scores, upper):
    rows = scores.shape[0] // 2
    down = lax.broadcasted_iota(jnp.int32, (rows, rows), 0)
    across = lax.broadcasted_iota(jnp.int32, (rows, rows), 1)
    late = across >= down
    blank = jnp.zeros((rows, rows), bf16)

    def corner(piece):
        weights = jnp.exp(piece)
        return (jnp.where(late, weights, 0.0) if upper else jnp.where(late, 0.0, weights)).astype(bf16)

    ends = (corner(scores[:rows, :rows]), corner(scores[rows:, rows:]))
    if upper:
        rest = jnp.exp(scores[:rows, rows:]).astype(bf16)
        lines = [[ends[0], rest], [blank, ends[1]]]
    else:
        rest = jnp.exp(scores[rows:, :rows]).astype(bf16)
        lines = [[ends[0], blank], [rest, ends[1]]]
    return jnp.concatenate([jnp.concatenate(line, axis=1) for line in lines], axis=0)


def attend_own(j, own, partial):
    rows, width = own.shape[0], own.shape[1] // 3
    half = rows // 2
    query = own[:, lane_block(j)]
    keys = own[:, lane_block(j + width // LANES)]
    values = own[:, lane_block(j + 2 * (width // LANES))]
    for head in range(2):
        scores = score(one_head(query, head), keys)
        early = [
            jnp.exp(scores[:half, :half]).astype(bf16), window_corner(scores[:half, half:], False),
        ]
        later = [
            window_corner(scores[half:, :half], True), jnp.exp(scores[half:, half:]).astype(bf16),
        ]
        weights = jnp.concatenate(
            [jnp.concatenate(early, axis=1), jnp.concatenate(later, axis=1)], axis=0
        )
        partial[2 * j + head] = jnp.dot(
            weights, with_counts(values, head, 1.0), preferred_element_type=f32
        )


def attend_beside(j, index, own, side, partial, attended, there):
    width = attended.shape[1]
    half = own.shape[0] // 2
    rows = slice(index * half, (index + 1) * half)
    query = own[rows, lane_block(j)]
    keys = side[rows, lane_block(j)]
    values = side[rows, lane_block(j + width // LANES)]
    totals = []
    for head in range(2):
        weights = window_corner(score(one_head(query, head), keys), index == 0)
        totals.append(
            jnp.dot(weights, with_counts(values, head, there), preferred_element_type=f32)
            + partial[2 * j + head, rows, :]
        )
    first = low_lanes()
    above = jnp.where(first, totals[0], totals[1])
    below = jnp.where(
        first, pltpu.roll(totals[0], HEAD_DIM, 1), pltpu.roll(totals[1], HEAD_DIM, 1)
    )
    attended[rows, lane_block(j)] = (above / below).astype(bf16)


def slope(diff):
    return diff * lax.rsqrt(diff * diff + smooth * smooth)


def copy_to(source, target, send, arrive, seq, member):
    return pltpu.make_async_remote_copy(
        src_ref=source,
        dst_ref=target,
        send_sem=send,
        recv_sem=arrive,
        device_id={"seq": seq, "member": member},
        device_id_type=pl.DeviceIdType.MESH,
    )


def layer_kernel(
    seqs, members, decoder, neighbours, area, tokens_far, weight_far, observed_far, output_far,
    middle_out, rows_out, decoder_out, joint,
    every, counts, turned, middle, edges, edges_in, terms, terms_in, sums, sums_in, mine,
    gathered_rows, gathered, tokens, attended, observed, output_weight,
    weight, normed, beside, own_parts, side_parts, mapped, partial, seen,
    halo_send, halo_in,
    local_sem, field_send, field_in, side_send, side_in, edge_send, edge_in, term_send, term_in,
    sum_send, sum_in, row_send, row_in, all_send, all_in,
):
    s, m = lax.axis_index("seq"), lax.axis_index("member")
    peers = seqs * members
    me = s * members + m
    tok_rows, fields = mapped.shape
    fan, grid_rows = neighbours.shape
    wide = tok_rows + 2 * REACH
    width = tokens.shape[1]
    chunk = width // peers

    def peer(step):
        flat = lax.rem(me + step, peers)
        return flat // members, lax.rem(flat, members)

    barrier = pltpu.get_barrier_semaphore()

    @pl.loop(1, peers)
    def _(step):
        seq, member = peer(step)
        pl.semaphore_signal(
            barrier, inc=1, device_id={"seq": seq, "member": member},
            device_id_type=pl.DeviceIdType.MESH,
        )

    columns = weight.shape[1] // COLS
    loads = [
        pltpu.make_async_copy(far, near, local_sem.at[i])
        for i, (far, near) in enumerate(
            [(tokens_far, tokens)]
            + [
                (weight_far.at[:, pl.ds(i * COLS, COLS)], weight.at[:, pl.ds(i * COLS, COLS)])
                for i in range(columns)
            ]
            + [(output_far, output_weight), (observed_far, observed)]
        )
    ]
    for load in loads:
        load.start()
    has_left, has_right = s > 0, s < seqs - 1
    half = WINDOW // 2

    def halo_copy(to_right):
        start, land, seq = (tok_rows - half, 0, s + 1) if to_right else (0, half, s - 1)
        return copy_to(
            tokens_far.at[pl.ds(start, half), :], beside.at[pl.ds(land, half), :],
            halo_send.at[to_right], halo_in.at[to_right], seq, m,
        )

    @pl.when(jnp.logical_not(has_left))
    def _():
        beside[:half, :] = jnp.zeros((half, width), bf16)

    @pl.when(jnp.logical_not(has_right))
    def _():
        beside[half:, :] = jnp.zeros((half, width), bf16)

    pl.semaphore_wait(barrier, peers - 1)

    @pl.when(has_right)
    def _():
        halo_copy(1).start()

    @pl.when(has_left)
    def _():
        halo_copy(0).start()

    loads[0].wait()
    normed[...] = normalize(tokens[...])
    project(normed, weight, own_parts, 0, loads[1 : 1 + columns])
    loads[1 + columns].wait()
    joint[...] = jnp.dot(
        output_weight[...], decoder[...], preferred_element_type=f32
    ).astype(bf16)
    mapped[...] = jnp.dot(tokens[...], decoder[...], preferred_element_type=f32)
    base = s * tok_rows - REACH
    block = 128
    loads[2 + columns].wait()

    @pl.loop(0, grid_rows // block)
    def _(i):
        cells = pl.ds(pl.multiple_of(i * block, block), block)
        local = neighbours[:, cells] - base
        place = lax.broadcasted_iota(jnp.int32, (wide, block), 0)
        total = jnp.zeros((wide, block), f32)
        for k in range(fan):
            total += jnp.where(local[k : k + 1, :] == place, 1.0 / fan, 0.0)
        counts[:, cells] = total.astype(bf16)
        seen[:, cells] = observed[cells, :].T

    blocks = width // LANES
    group = math.gcd(blocks, 4)

    @pl.loop(0, blocks // group)
    def _(i):
        for k in range(group):
            attend_own(i * group + k, own_parts, partial)

    @pl.when(has_left)
    def _():
        halo_copy(0).wait_send()
        halo_copy(1).wait_recv()

    @pl.when(has_right)
    def _():
        halo_copy(1).wait_send()
        halo_copy(0).wait_recv()

    normed[...] = normalize(beside[...])
    project(normed, weight, side_parts, width, None)
    def field_copy(index, step):
        cells = pl.ds(REACH + index * half, half)
        return copy_to(
            every.at[pl.ds(0, fields), cells], every.at[pl.ds(step * fields, fields), cells],
            field_send.at[index, step], field_in.at[index, step], s, lax.rem(m + step, members),
        )

    def side_copy(side, step):
        start, land, seq = ((tok_rows, 0, s + 1), (REACH, REACH + tok_rows, s - 1))[side]
        return copy_to(
            every.at[pl.ds(0, fields), pl.ds(start, REACH)],
            every.at[pl.ds(step * fields, fields), pl.ds(land, REACH)],
            side_send.at[side, step], side_in.at[side, step], seq, lax.rem(m + step, members),
        )

    for index in range(2):
        there = jnp.where((has_left, has_right)[index], 1.0, 0.0).astype(f32)
        for j in range(blocks):
            attend_beside(j, index, own_parts, side_parts, partial, attended, there)
        at = index * half
        total = mapped[at : at + half, :] + jnp.dot(
            attended[at : at + half, :], joint[...], preferred_element_type=f32
        )
        every[:fields, REACH + at : REACH + at + half] = total.T.astype(bf16)
        for step in range(1, members):
            field_copy(index, step).start()

        @pl.when((has_left, has_right)[index])
        def _():
            for step in range(members):
                side_copy(1 - index, step).start()

    @pl.when(jnp.logical_not(has_left))
    def _():
        every[:, :REACH] = jnp.zeros((members * fields, REACH), bf16)
        edges_in[0] = jnp.zeros((fields, REACH), bf16)

    @pl.when(jnp.logical_not(has_right))
    def _():
        every[:, wide - REACH :] = jnp.zeros((members * fields, REACH), bf16)
        edges_in[1] = jnp.zeros((fields, REACH), bf16)

    for index in range(2):
        for step in range(1, members):
            field_copy(index, step).wait()

    @pl.when(has_left)
    def _():
        for step in range(members):
            side_copy(1, step).wait_send()
            side_copy(0, step).wait_recv()

    @pl.when(has_right)
    def _():
        for step in range(members):
            side_copy(0, step).wait_send()
            side_copy(1, step).wait_recv()

    block = 256

    @pl.loop(0, grid_rows // block)
    def _(i):
        cells = pl.ds(pl.multiple_of(i * block, block), block)
        found = jnp.dot(every[...], counts[:, cells], preferred_element_type=f32)
        mean = found[:fields, :]
        pairs = jnp.zeros((fields, block), f32)
        for step in range(members):
            pairs += slope(mean - found[step * fields : (step + 1) * fields, :])
        single = slope(mean - seen[:, cells])
        turned[:, cells] = (
            area[:, cells]
            * (single * (1.0 / members) - pairs * (1.0 / (members * (members - 1))))
        ).astype(bf16)

    def spread(start, size):
        return lax.dot_general(
            turned[...], counts[start : start + size, :], (((1,), (1,)), ((), ())),
            preferred_element_type=f32,
        )

    edges[0] = spread(0, REACH).astype(bf16)
    edges[1] = spread(REACH + tok_rows, REACH).astype(bf16)

    def edge_copy(side):
        return copy_to(
            edges.at[side], edges_in.at[1 - side], edge_send.at[side], edge_in.at[side],
            s - 1 if side == 0 else s + 1, m,
        )

    @pl.when(has_left)
    def _():
        edge_copy(0).start()

    @pl.when(has_right)
    def _():
        edge_copy(1).start()

    middle[...] = spread(REACH, tok_rows)
    inner = middle[:, REACH : tok_rows - REACH].astype(bf16)
    output_term = jnp.dot(
        inner, attended[REACH : tok_rows - REACH, :], preferred_element_type=f32
    )

    @pl.when(has_left)
    def _():
        edge_copy(0).wait_send()
        edge_copy(1).wait_recv()

    @pl.when(has_right)
    def _():
        edge_copy(1).wait_send()
        edge_copy(0).wait_recv()

    middle[:, :REACH] += edges_in[0].astype(f32)
    middle[:, tok_rows - REACH :] += edges_in[1].astype(f32)
    whole = middle[...].astype(bf16)
    output_term += jnp.dot(whole[:, :REACH], attended[:REACH, :], preferred_element_type=f32)
    output_term += jnp.dot(
        whole[:, tok_rows - REACH :], attended[tok_rows - REACH :, :],
        preferred_element_type=f32,
    )

    def put(part, value):
        rows = value.T.astype(bf16)
        for member in range(members):
            for seq in range(seqs):
                at = (seq * members + member) * chunk
                terms[part, member, seq] = rows[at : at + chunk, :]

    def term_copy(part, step):
        member = lax.rem(m + step, members)
        return copy_to(
            terms.at[part, member], terms_in.at[part, step],
            term_send.at[part, step], term_in.at[part, step], s, member,
        )

    def sum_copy(part, step):
        seq = lax.rem(s + step, seqs)
        return copy_to(
            sums.at[part, seq], sums_in.at[part, step],
            sum_send.at[part, step], sum_in.at[part, step], seq, m,
        )

    put(0, output_term)
    for step in range(1, members):
        term_copy(0, step).start()
    decoder_term = jnp.dot(whole, tokens[...], preferred_element_type=f32)
    decoder_term += jnp.dot(
        output_term.astype(bf16), output_weight[...], preferred_element_type=f32
    )
    put(1, decoder_term)
    for step in range(1, members):
        term_copy(1, step).start()
    middle_out[...] = middle[...].T.astype(bf16)
    for part in range(2):
        for step in range(1, members):
            term_copy(part, step).wait()
        total = terms[part, m].astype(f32)
        for step in range(1, members):
            total += terms_in[part, step].astype(f32)
        sums[part] = total.astype(bf16)

        @pl.loop(1, seqs)
        def _(step):
            sum_copy(part, step).start()

    def row_copy(step):
        return copy_to(
            mine.at[0], gathered_rows.at[m], row_send.at[step], row_in.at[step],
            s, lax.rem(m + step, members),
        )

    def all_copy(step):
        seq, member = peer(step)
        return copy_to(
            mine.at[1], gathered.at[me], all_send.at[step], all_in.at[step], seq, member
        )

    for part in range(2):

        @pl.loop(1, seqs)
        def _(step):
            sum_copy(part, step).wait()

        total = sums[part, s].astype(f32)
        for step in range(1, seqs):
            total += sums_in[part, step].astype(f32)
        mine[part] = total.astype(bf16)
        if part == 0:
            for step in range(1, members):
                row_copy(step).start()
        else:

            @pl.loop(1, peers)
            def _(step):
                all_copy(step).start()

    gathered_rows[m] = mine[0]
    gathered[me] = mine[1]
    for step in range(1, members):
        row_copy(step).wait()
    rows_out[...] = gathered_rows[...]

    @pl.loop(1, peers)
    def _(step):
        all_copy(step).wait()

    decoder_out[...] = gathered[...]


def layer(decoder, neighbours, area, tokens, weight, observed, output_weight, seqs, members):
    tok_rows, width = tokens.shape
    fields = decoder.shape[1]
    grid_rows = neighbours.shape[1]
    wide = tok_rows + 2 * REACH
    peers = seqs * members
    chunk = width // peers
    near = pl.BlockSpec(memory_space=pltpu.VMEM)
    far = pl.BlockSpec(memory_space=pl.ANY)
    dma = pltpu.SemaphoreType.DMA
    return pl.pallas_call(
        functools.partial(layer_kernel, seqs, members),
        in_specs=[near] * 3 + [far] * 4,
        out_specs=[near] * 4,
        out_shape=[
            pltpu.VMEM((tok_rows, fields), bf16),
            pltpu.VMEM((members, chunk, fields), bf16),
            pltpu.VMEM((peers, chunk, fields), bf16),
            pltpu.VMEM((width, fields), bf16),
        ],
        scratch_shapes=[
            pltpu.VMEM((members * fields, wide), bf16),
            pltpu.VMEM((wide, grid_rows), bf16),
            pltpu.VMEM((fields, grid_rows), bf16),
            pltpu.VMEM((fields, tok_rows), f32),
            pltpu.VMEM((2, fields, REACH), bf16),
            pltpu.VMEM((2, fields, REACH), bf16),
            pltpu.VMEM((2, members, seqs, chunk, fields), bf16),
            pltpu.VMEM((2, members, seqs, chunk, fields), bf16),
            pltpu.VMEM((2, seqs, chunk, fields), bf16),
            pltpu.VMEM((2, seqs, chunk, fields), bf16),
            pltpu.VMEM((2, chunk, fields), bf16),
            pltpu.VMEM((members, chunk, fields), bf16),
            pltpu.VMEM((peers, chunk, fields), bf16),
            pltpu.VMEM(tokens.shape, bf16),
            pltpu.VMEM(tokens.shape, bf16),
            pltpu.VMEM(observed.shape, f32),
            pltpu.VMEM(output_weight.shape, bf16),
            pltpu.VMEM(weight.shape, bf16),
            pltpu.VMEM(tokens.shape, bf16),
            pltpu.VMEM((WINDOW, width), bf16),
            pltpu.VMEM((tok_rows, 3 * width), bf16),
            pltpu.VMEM((WINDOW, 2 * width), bf16),
            pltpu.VMEM((tok_rows, fields), f32),
            pltpu.VMEM((2 * (width // LANES), tok_rows, LANES), f32),
            pltpu.VMEM((fields, grid_rows), f32),
            dma((2,)),
            dma((2,)),
            dma((3 + weight.shape[1] // COLS,)),
            dma((2, members)),
            dma((2, members)),
            dma((2, members)),
            dma((2, members)),
            dma((2,)),
            dma((2,)),
            dma((2, members)),
            dma((2, members)),
            dma((2, seqs)),
            dma((2, seqs)),
            dma((members,)),
            dma((members,)),
            dma((peers,)),
            dma((peers,)),
        ],
        compiler_params=pltpu.CompilerParams(
            vmem_limit_bytes=56 << 20, collective_id=0, has_side_effects=True
        ),
    )(decoder, neighbours, area, tokens, weight, observed, output_weight)


def finish_kernel(
    output_scale, decoder_scale, middle, joint, rows, decoder, decoder_sum,
    cotangent_far, output_far, decoder_far, cotangent, output, decoder_near, sems,
):
    copies = []

    def send(near, far, part):
        copy = pltpu.make_async_copy(near.at[part], far.at[part], sems.at[len(copies)])
        copy.start()
        copies.append(copy)

    decoder_near[...] = decoder_sum[...].reshape(decoder.shape).astype(f32) * decoder_scale
    send(decoder_near, decoder_far, slice(None))
    output[...] = score(rows[...].reshape(output.shape[0], -1), decoder[...]) * output_scale
    send(output, output_far, slice(None))
    size = cotangent.shape[0] // 2
    for part in range(2):
        at = slice(part * size, (part + 1) * size)
        cotangent[at, :] = score(middle[at, :], joint[...]).astype(bf16)
        send(cotangent, cotangent_far, pl.ds(part * size, size))
    for copy in copies:
        copy.wait()


def finish(middle, joint, rows, decoder, decoder_sum, output_scale, decoder_scale):
    width, fields = decoder.shape
    shapes = [
        jax.ShapeDtypeStruct((middle.shape[0], width), bf16),
        jax.ShapeDtypeStruct((rows.shape[0] * rows.shape[1], width), f32),
        jax.ShapeDtypeStruct((width, fields), f32),
    ]
    return pl.pallas_call(
        functools.partial(finish_kernel, output_scale, decoder_scale),
        in_specs=[pl.BlockSpec(memory_space=pltpu.VMEM)] * 5,
        out_specs=[pl.BlockSpec(memory_space=pl.ANY)] * 3,
        out_shape=shapes,
        scratch_shapes=[pltpu.VMEM(shape.shape, shape.dtype) for shape in shapes]
        + [pltpu.SemaphoreType.DMA((4,))],
        compiler_params=pltpu.CompilerParams(vmem_limit_bytes=16 << 20),
    )(middle, joint, rows, decoder, decoder_sum)


def body(tokens, input_weight, output_weight, decoder_weight, neighbours, observed, cell_area):
    own_tokens = tokens[0]
    tok_rows, width = own_tokens.shape
    fields = decoder_weight.shape[1]
    seqs = lax.axis_size("seq")
    members = lax.axis_size("member")
    grid_rows = neighbours.shape[0]
    middle, rows, decoder_sum, joint = layer(
        decoder_weight, neighbours.T, cell_area[None, :], own_tokens, input_weight, observed,
        output_weight, seqs, members,
    )
    attention_cotangent, output_gradient, decoder_gradient = finish(
        middle, joint, rows, decoder_weight, decoder_sum,
        1.0 / math.sqrt(members * tok_rows * seqs), 1.0 / math.sqrt(members * grid_rows * seqs),
    )
    return (attention_cotangent[None], output_gradient, decoder_gradient)


def solution(mesh):
    in_specs = (
        P(("group", "member"), "seq", None),
        P(),
        P(),
        P(),
        P("seq", None),
        P(("group", "seq"), None),
        P("seq"),
    )
    out_specs = (P(("group", "member"), "seq", None), P(("group", "seq"), None), P("group", None))
    return jax.shard_map(body, mesh=mesh, in_specs=in_specs, out_specs=out_specs, check_vma=False)
```

```python
import functools
import math

import jax
import jax.numpy as jnp
from jax import lax
from jax.experimental import pallas as pl
from jax.experimental.pallas import tpu as pltpu
from jax.sharding import PartitionSpec as P

HEAD_DIM = 64
WINDOW = 512
REACH = 128
LANES = 128
COLS = 512

smooth = 0.1
f32 = jnp.float32
bf16 = jnp.bfloat16


def normalize(rows):
    values = rows.astype(f32)
    centre = jnp.mean(values, axis=-1, keepdims=True)
    values = values - centre
    spread = jnp.mean(values * values, axis=-1, keepdims=True)
    return (values * lax.rsqrt(spread + 1e-05)).astype(bf16)


def place_columns(mixed, scale):
    side = 256
    down = lax.broadcasted_iota(jnp.int32, (side, side), 0) >> 6
    across = lax.broadcasted_iota(jnp.int32, (side, side), 1) >> 6
    same = jnp.where(down == across, 1.0 / HEAD_DIM, 0.0).astype(bf16)
    pieces = []
    for at in range(0, mixed.shape[1], side):
        piece = mixed[:, at : at + side]
        mean = jnp.dot((piece * piece).astype(bf16), same, preferred_element_type=f32)
        pieces.append((piece * (lax.rsqrt(mean + 1e-06) * scale)).astype(bf16))
    return jnp.concatenate(pieces, axis=1)


def project(normed, weight, out, first, waits):
    width = weight.shape[0]
    for at in range(first, weight.shape[1], COLS):
        if waits:
            waits[at // COLS].wait()
        mixed = jnp.dot(normed[...], weight[:, at : at + COLS], preferred_element_type=f32)
        if at < 2 * width:
            mixed = place_columns(mixed, HEAD_DIM**-0.5 if at < width else 1.0)
        out[:, at - first : at - first + COLS] = mixed.astype(bf16)


def lane_block(j):
    return pl.ds(pl.multiple_of(j * LANES, LANES), LANES)


def low_lanes():
    return lax.broadcasted_iota(jnp.int32, (1, LANES), 1) < HEAD_DIM


def one_head(pair, head):
    return jnp.where(low_lanes() == (head == 0), pair, jnp.zeros_like(pair))


def with_counts(pair, head, real):
    ones = jnp.full(pair.shape, real, f32).astype(bf16)
    first = low_lanes()
    return jnp.where(first, pair, ones) if head == 0 else jnp.where(first, ones, pair)


def score(query, keys):
    return lax.dot_general(query, keys, (((1,), (1,)), ((), ())), preferred_element_type=f32)


def window_corner(scores, upper):
    rows = scores.shape[0] // 2
    down = lax.broadcasted_iota(jnp.int32, (rows, rows), 0)
    across = lax.broadcasted_iota(jnp.int32, (rows, rows), 1)
    late = across >= down
    blank = jnp.zeros((rows, rows), bf16)

    def corner(piece):
        weights = jnp.exp(piece)
        return (jnp.where(late, weights, 0.0) if upper else jnp.where(late, 0.0, weights)).astype(bf16)

    ends = (corner(scores[:rows, :rows]), corner(scores[rows:, rows:]))
    if upper:
        rest = jnp.exp(scores[:rows, rows:]).astype(bf16)
        lines = [[ends[0], rest], [blank, ends[1]]]
    else:
        rest = jnp.exp(scores[rows:, :rows]).astype(bf16)
        lines = [[ends[0], blank], [rest, ends[1]]]
    return jnp.concatenate([jnp.concatenate(line, axis=1) for line in lines], axis=0)


def attend_own(j, own, partial):
    rows, width = own.shape[0], own.shape[1] // 3
    half = rows // 2
    query = own[:, lane_block(j)]
    keys = own[:, lane_block(j + width // LANES)]
    values = own[:, lane_block(j + 2 * (width // LANES))]
    for head in range(2):
        scores = score(one_head(query, head), keys)
        early = [
            jnp.exp(scores[:half, :half]).astype(bf16), window_corner(scores[:half, half:], False),
        ]
        later = [
            window_corner(scores[half:, :half], True), jnp.exp(scores[half:, half:]).astype(bf16),
        ]
        weights = jnp.concatenate(
            [jnp.concatenate(early, axis=1), jnp.concatenate(later, axis=1)], axis=0
        )
        partial[2 * j + head] = jnp.dot(
            weights, with_counts(values, head, 1.0), preferred_element_type=f32
        )


def attend_beside(j, index, own, side, partial, attended, there):
    width = attended.shape[1]
    half = own.shape[0] // 2
    rows = slice(index * half, (index + 1) * half)
    query = own[rows, lane_block(j)]
    keys = side[rows, lane_block(j)]
    values = side[rows, lane_block(j + width // LANES)]
    totals = []
    for head in range(2):
        weights = window_corner(score(one_head(query, head), keys), index == 0)
        totals.append(
            jnp.dot(weights, with_counts(values, head, there), preferred_element_type=f32)
            + partial[2 * j + head, rows, :]
        )
    first = low_lanes()
    above = jnp.where(first, totals[0], totals[1])
    below = jnp.where(
        first, pltpu.roll(totals[0], HEAD_DIM, 1), pltpu.roll(totals[1], HEAD_DIM, 1)
    )
    attended[rows, lane_block(j)] = (above / below).astype(bf16)


def slope(diff):
    return diff * lax.rsqrt(diff * diff + smooth * smooth)


def copy_to(source, target, send, arrive, seq, member):
    return pltpu.make_async_remote_copy(
        src_ref=source,
        dst_ref=target,
        send_sem=send,
        recv_sem=arrive,
        device_id={"seq": seq, "member": member},
        device_id_type=pl.DeviceIdType.MESH,
    )


def layer_kernel(
    seqs, members, decoder, neighbours, area, tokens_far, weight_far, observed_far, output_far,
    middle_out, rows_out, decoder_out, joint,
    every, counts, turned, middle, edges, edges_in, terms, terms_in, pair, pair_in,
    sums, sums_in, mine,
    gathered_rows, gathered, tokens, attended, observed, output_weight,
    weight, normed, beside, own_parts, side_parts, mapped, partial, seen,
    halo_send, halo_in,
    local_sem, field_send, field_in, side_send, side_in, edge_send, edge_in, core_send, core_in,
    term_send, term_in,
    sum_send, sum_in, row_send, row_in, all_send, all_in,
):
    s, m = lax.axis_index("seq"), lax.axis_index("member")
    peers = seqs * members
    me = s * members + m
    ranks, x, c = members // 2, m // 2, lax.rem(m, 2)
    sibling = m + 1 - 2 * c
    tok_rows, fields = mapped.shape
    fan, grid_rows = neighbours.shape
    wide = tok_rows + 2 * REACH
    width = tokens.shape[1]
    chunk = width // peers

    def peer(step):
        flat = lax.rem(me + step, peers)
        return flat // members, lax.rem(flat, members)

    barrier = pltpu.get_barrier_semaphore()

    @pl.loop(1, peers)
    def _(step):
        seq, member = peer(step)
        pl.semaphore_signal(
            barrier, inc=1, device_id={"seq": seq, "member": member},
            device_id_type=pl.DeviceIdType.MESH,
        )

    columns = weight.shape[1] // COLS
    loads = [
        pltpu.make_async_copy(far, near, local_sem.at[i])
        for i, (far, near) in enumerate(
            [(tokens_far, tokens)]
            + [
                (weight_far.at[:, pl.ds(i * COLS, COLS)], weight.at[:, pl.ds(i * COLS, COLS)])
                for i in range(columns)
            ]
            + [(output_far, output_weight), (observed_far, observed)]
        )
    ]
    for load in loads:
        load.start()
    has_left, has_right = s > 0, s < seqs - 1
    half = WINDOW // 2

    def halo_copy(to_right):
        start, land, seq = (tok_rows - half, 0, s + 1) if to_right else (0, half, s - 1)
        return copy_to(
            tokens_far.at[pl.ds(start, half), :], beside.at[pl.ds(land, half), :],
            halo_send.at[to_right], halo_in.at[to_right], seq, m,
        )

    @pl.when(jnp.logical_not(has_left))
    def _():
        beside[:half, :] = jnp.zeros((half, width), bf16)

    @pl.when(jnp.logical_not(has_right))
    def _():
        beside[half:, :] = jnp.zeros((half, width), bf16)

    pl.semaphore_wait(barrier, peers - 1)

    @pl.when(has_right)
    def _():
        halo_copy(1).start()

    @pl.when(has_left)
    def _():
        halo_copy(0).start()

    loads[0].wait()
    normed[...] = normalize(tokens[...])
    project(normed, weight, own_parts, 0, loads[1 : 1 + columns])
    loads[1 + columns].wait()
    joint[...] = jnp.dot(
        output_weight[...], decoder[...], preferred_element_type=f32
    ).astype(bf16)
    mapped[...] = jnp.dot(tokens[...], decoder[...], preferred_element_type=f32)
    base = s * tok_rows - REACH
    block = 128
    loads[2 + columns].wait()

    @pl.loop(0, grid_rows // block)
    def _(i):
        cells = pl.ds(pl.multiple_of(i * block, block), block)
        local = neighbours[:, cells] - base
        place = lax.broadcasted_iota(jnp.int32, (wide, block), 0)
        total = jnp.zeros((wide, block), f32)
        for k in range(fan):
            total += jnp.where(local[k : k + 1, :] == place, 1.0 / fan, 0.0)
        counts[:, cells] = total.astype(bf16)
        seen[:, cells] = observed[cells, :].T

    blocks = width // LANES
    group = math.gcd(blocks, 4)

    @pl.loop(0, blocks // group)
    def _(i):
        for k in range(group):
            attend_own(i * group + k, own_parts, partial)

    @pl.when(has_left)
    def _():
        halo_copy(0).wait_send()
        halo_copy(1).wait_recv()

    @pl.when(has_right)
    def _():
        halo_copy(1).wait_send()
        halo_copy(0).wait_recv()

    normed[...] = normalize(beside[...])
    project(normed, weight, side_parts, width, None)
    bands = (
        (REACH, half), (REACH + half, half), (0, REACH), (REACH + tok_rows, REACH),
    )

    def field_copy(core, band, step):
        start, size = bands[band]
        cells = pl.ds(start, size)
        here = step if core else 0
        there = ranks * core + step
        member = sibling if core else 2 * lax.rem(x + step, ranks) + c
        return copy_to(
            every.at[pl.ds(here * fields, fields), cells],
            every.at[pl.ds(there * fields, fields), cells],
            field_send.at[band, there], field_in.at[band, there], s, member,
        )

    def side_copy(side):
        start, land, seq = ((tok_rows, 0, s + 1), (REACH, REACH + tok_rows, s - 1))[side]
        return copy_to(
            every.at[pl.ds(0, fields), pl.ds(start, REACH)],
            every.at[pl.ds(0, fields), pl.ds(land, REACH)],
            side_send.at[side], side_in.at[side], seq, m,
        )

    def share(band):
        for step in range(1, ranks):
            field_copy(0, band, step).start()
        field_copy(1, band, 0).start()

    def forward(band):
        for step in range(1, ranks):
            field_copy(0, band, step).wait_recv()
            field_copy(1, band, step).start()

    def settle(band):
        for step in range(1, ranks):
            field_copy(0, band, step).wait_send()
        for step in range(ranks):
            field_copy(1, band, step).wait()

    for index in range(2):
        there = jnp.where((has_left, has_right)[index], 1.0, 0.0).astype(f32)
        for j in range(blocks):
            attend_beside(j, index, own_parts, side_parts, partial, attended, there)
        at = index * half
        total = mapped[at : at + half, :] + jnp.dot(
            attended[at : at + half, :], joint[...], preferred_element_type=f32
        )
        every[:fields, REACH + at : REACH + at + half] = total.T.astype(bf16)
        share(index)

        @pl.when((has_left, has_right)[index])
        def _():
            side_copy(1 - index).start()

    @pl.when(jnp.logical_not(has_left))
    def _():
        every[:, :REACH] = jnp.zeros((members * fields, REACH), bf16)
        edges_in[0] = jnp.zeros((fields, REACH), bf16)

    @pl.when(jnp.logical_not(has_right))
    def _():
        every[:, wide - REACH :] = jnp.zeros((members * fields, REACH), bf16)
        edges_in[1] = jnp.zeros((fields, REACH), bf16)

    @pl.when(has_right)
    def _():
        side_copy(1).wait_recv()
        share(3)

    forward(0)

    @pl.when(has_left)
    def _():
        side_copy(0).wait_recv()
        share(2)

    forward(1)

    @pl.when(has_right)
    def _():
        forward(3)
        side_copy(0).wait_send()

    @pl.when(has_left)
    def _():
        forward(2)
        side_copy(1).wait_send()

    settle(0)
    settle(1)

    @pl.when(has_right)
    def _():
        settle(3)

    @pl.when(has_left)
    def _():
        settle(2)

    block = 256

    @pl.loop(0, grid_rows // block)
    def _(i):
        cells = pl.ds(pl.multiple_of(i * block, block), block)
        found = jnp.dot(every[...], counts[:, cells], preferred_element_type=f32)
        mean = found[:fields, :]
        pairs = jnp.zeros((fields, block), f32)
        for step in range(1, members):
            pairs += slope(mean - found[step * fields : (step + 1) * fields, :])
        single = slope(mean - seen[:, cells])
        turned[:, cells] = (
            area[:, cells]
            * (single * (1.0 / members) - pairs * (1.0 / (members * (members - 1))))
        ).astype(bf16)

    def spread(start, size):
        return lax.dot_general(
            turned[...], counts[start : start + size, :], (((1,), (1,)), ((), ())),
            preferred_element_type=f32,
        )

    edges[0] = spread(0, REACH).astype(bf16)
    edges[1] = spread(REACH + tok_rows, REACH).astype(bf16)

    def edge_copy(side):
        return copy_to(
            edges.at[side], edges_in.at[1 - side], edge_send.at[side], edge_in.at[side],
            s - 1 if side == 0 else s + 1, m,
        )

    @pl.when(has_left)
    def _():
        edge_copy(0).start()

    @pl.when(has_right)
    def _():
        edge_copy(1).start()

    middle[...] = spread(REACH, tok_rows)
    inner = middle[:, REACH : tok_rows - REACH].astype(bf16)
    output_term = jnp.dot(
        inner, attended[REACH : tok_rows - REACH, :], preferred_element_type=f32
    )

    @pl.when(has_left)
    def _():
        edge_copy(0).wait_send()
        edge_copy(1).wait_recv()

    @pl.when(has_right)
    def _():
        edge_copy(1).wait_send()
        edge_copy(0).wait_recv()

    middle[:, :REACH] += edges_in[0].astype(f32)
    middle[:, tok_rows - REACH :] += edges_in[1].astype(f32)
    whole = middle[...].astype(bf16)
    output_term += jnp.dot(whole[:, :REACH], attended[:REACH, :], preferred_element_type=f32)
    output_term += jnp.dot(
        whole[:, tok_rows - REACH :], attended[tok_rows - REACH :, :],
        preferred_element_type=f32,
    )

    spots = seqs * ranks
    spot = s * ranks + x

    def put(part, value):
        rows = value.T.astype(bf16)
        for core in range(2):
            for rank in range(ranks):
                for seq in range(seqs):
                    at = (seq * members + 2 * rank + core) * chunk
                    terms[part, core, rank, seq] = rows[at : at + chunk, :]

    def core_copy(part):
        return copy_to(
            terms.at[part, 1 - c], terms_in.at[part], core_send.at[part], core_in.at[part],
            s, sibling,
        )

    def rank_copy(part, step):
        rank = lax.rem(x + step, ranks)
        return copy_to(
            pair.at[part, rank], pair_in.at[part, step],
            term_send.at[part, step], term_in.at[part, step], s, 2 * rank + c,
        )

    def sum_copy(part, step):
        seq = lax.rem(s + step, seqs)
        return copy_to(
            sums.at[part, seq], sums_in.at[part, step],
            sum_send.at[part, step], sum_in.at[part, step], seq, m,
        )

    def row_copy(step):
        return copy_to(
            mine.at[0], gathered_rows.at[m], row_send.at[step], row_in.at[step],
            s, lax.rem(m + step, members),
        )

    def all_copy(step):
        other = lax.rem(spot + step, spots)
        return copy_to(
            mine.at[1], gathered.at[c, spot], all_send.at[step], all_in.at[step],
            other // ranks, 2 * lax.rem(other, ranks) + c,
        )

    def last_copy():
        return copy_to(
            gathered.at[c], gathered.at[c], core_send.at[2], core_in.at[2], s, sibling
        )

    def add_cores(part):
        core_copy(part).wait()
        pair[part] = (terms[part, c].astype(f32) + terms_in[part].astype(f32)).astype(bf16)
        for step in range(1, ranks):
            rank_copy(part, step).start()

    def add_ranks(part):
        for step in range(1, ranks):
            rank_copy(part, step).wait()
        total = pair[part, x].astype(f32)
        for step in range(1, ranks):
            total += pair_in[part, step].astype(f32)
        sums[part] = total.astype(bf16)

        @pl.loop(1, seqs)
        def _(step):
            sum_copy(part, step).start()

    def add_seqs(part):
        @pl.loop(1, seqs)
        def _(step):
            sum_copy(part, step).wait()

        total = sums[part, s].astype(f32)
        for step in range(1, seqs):
            total += sums_in[part, step].astype(f32)
        mine[part] = total.astype(bf16)

    put(0, output_term)
    core_copy(0).start()
    decoder_term = jnp.dot(whole, tokens[...], preferred_element_type=f32)
    add_cores(0)
    decoder_term += jnp.dot(
        output_term.astype(bf16), output_weight[...], preferred_element_type=f32
    )
    put(1, decoder_term)
    core_copy(1).start()
    middle_out[...] = middle[...].T.astype(bf16)
    add_cores(1)
    add_ranks(0)
    add_ranks(1)
    add_seqs(0)
    for step in range(1, members):
        row_copy(step).start()
    gathered_rows[m] = mine[0]
    add_seqs(1)

    @pl.loop(1, spots)
    def _(step):
        all_copy(step).start()

    gathered[c, spot] = mine[1]
    for step in range(1, members):
        row_copy(step).wait()
    rows_out[...] = gathered_rows[...]

    @pl.loop(1, spots)
    def _(step):
        all_copy(step).wait()

    last_copy().start()
    last_copy().wait()
    decoder_out[...] = gathered[...]


def layer(decoder, neighbours, area, tokens, weight, observed, output_weight, seqs, members):
    tok_rows, width = tokens.shape
    fields = decoder.shape[1]
    grid_rows = neighbours.shape[1]
    wide = tok_rows + 2 * REACH
    ranks = members // 2
    chunk = width // (seqs * members)
    near = pl.BlockSpec(memory_space=pltpu.VMEM)
    far = pl.BlockSpec(memory_space=pl.ANY)
    dma = pltpu.SemaphoreType.DMA
    return pl.pallas_call(
        functools.partial(layer_kernel, seqs, members),
        in_specs=[near] * 3 + [far] * 4,
        out_specs=[near] * 4,
        out_shape=[
            pltpu.VMEM((tok_rows, fields), bf16),
            pltpu.VMEM((members, chunk, fields), bf16),
            pltpu.VMEM((2, seqs * ranks, chunk, fields), bf16),
            pltpu.VMEM((width, fields), bf16),
        ],
        scratch_shapes=[
            pltpu.VMEM((members * fields, wide), bf16),
            pltpu.VMEM((wide, grid_rows), bf16),
            pltpu.VMEM((fields, grid_rows), bf16),
            pltpu.VMEM((fields, tok_rows), f32),
            pltpu.VMEM((2, fields, REACH), bf16),
            pltpu.VMEM((2, fields, REACH), bf16),
            pltpu.VMEM((2, 2, ranks, seqs, chunk, fields), bf16),
            pltpu.VMEM((2, ranks, seqs, chunk, fields), bf16),
            pltpu.VMEM((2, ranks, seqs, chunk, fields), bf16),
            pltpu.VMEM((2, ranks, seqs, chunk, fields), bf16),
            pltpu.VMEM((2, seqs, chunk, fields), bf16),
            pltpu.VMEM((2, seqs, chunk, fields), bf16),
            pltpu.VMEM((2, chunk, fields), bf16),
            pltpu.VMEM((members, chunk, fields), bf16),
            pltpu.VMEM((2, seqs * ranks, chunk, fields), bf16),
            pltpu.VMEM(tokens.shape, bf16),
            pltpu.VMEM(tokens.shape, bf16),
            pltpu.VMEM(observed.shape, f32),
            pltpu.VMEM(output_weight.shape, bf16),
            pltpu.VMEM(weight.shape, bf16),
            pltpu.VMEM(tokens.shape, bf16),
            pltpu.VMEM((WINDOW, width), bf16),
            pltpu.VMEM((tok_rows, 3 * width), bf16),
            pltpu.VMEM((WINDOW, 2 * width), bf16),
            pltpu.VMEM((tok_rows, fields), f32),
            pltpu.VMEM((2 * (width // LANES), tok_rows, LANES), f32),
            pltpu.VMEM((fields, grid_rows), f32),
            dma((2,)),
            dma((2,)),
            dma((3 + weight.shape[1] // COLS,)),
            dma((4, members)),
            dma((4, members)),
            dma((2,)),
            dma((2,)),
            dma((2,)),
            dma((2,)),
            dma((3,)),
            dma((3,)),
            dma((2, ranks)),
            dma((2, ranks)),
            dma((2, seqs)),
            dma((2, seqs)),
            dma((members,)),
            dma((members,)),
            dma((seqs * ranks,)),
            dma((seqs * ranks,)),
        ],
        compiler_params=pltpu.CompilerParams(
            vmem_limit_bytes=56 << 20, collective_id=0, has_side_effects=True
        ),
    )(decoder, neighbours, area, tokens, weight, observed, output_weight)


def finish_kernel(
    output_scale, decoder_scale, middle, joint, rows, decoder, decoder_sum,
    cotangent_far, output_far, decoder_far, cotangent, output, decoder_near, sems,
):
    copies = []

    def send(near, far, part):
        copy = pltpu.make_async_copy(near.at[part], far.at[part], sems.at[len(copies)])
        copy.start()
        copies.append(copy)

    cores, spots, chunk, _ = decoder_sum.shape
    for spot in range(spots):
        for core in range(cores):
            at = (cores * spot + core) * chunk
            decoder_near[at : at + chunk, :] = decoder_sum[core, spot].astype(f32) * decoder_scale
    send(decoder_near, decoder_far, slice(None))
    output[...] = score(rows[...].reshape(output.shape[0], -1), decoder[...]) * output_scale
    send(output, output_far, slice(None))
    size = cotangent.shape[0] // 2
    for part in range(2):
        at = slice(part * size, (part + 1) * size)
        cotangent[at, :] = score(middle[at, :], joint[...]).astype(bf16)
        send(cotangent, cotangent_far, pl.ds(part * size, size))
    for copy in copies:
        copy.wait()


def finish(middle, joint, rows, decoder, decoder_sum, output_scale, decoder_scale):
    width, fields = decoder.shape
    shapes = [
        jax.ShapeDtypeStruct((middle.shape[0], width), bf16),
        jax.ShapeDtypeStruct((rows.shape[0] * rows.shape[1], width), f32),
        jax.ShapeDtypeStruct((width, fields), f32),
    ]
    return pl.pallas_call(
        functools.partial(finish_kernel, output_scale, decoder_scale),
        in_specs=[pl.BlockSpec(memory_space=pltpu.VMEM)] * 5,
        out_specs=[pl.BlockSpec(memory_space=pl.ANY)] * 3,
        out_shape=shapes,
        scratch_shapes=[pltpu.VMEM(shape.shape, shape.dtype) for shape in shapes]
        + [pltpu.SemaphoreType.DMA((4,))],
        compiler_params=pltpu.CompilerParams(vmem_limit_bytes=16 << 20),
    )(middle, joint, rows, decoder, decoder_sum)


def body(tokens, input_weight, output_weight, decoder_weight, neighbours, observed, cell_area):
    own_tokens = tokens[0]
    tok_rows, width = own_tokens.shape
    fields = decoder_weight.shape[1]
    seqs = lax.axis_size("seq")
    members = lax.axis_size("member")
    grid_rows = neighbours.shape[0]
    middle, rows, decoder_sum, joint = layer(
        decoder_weight, neighbours.T, cell_area[None, :], own_tokens, input_weight, observed,
        output_weight, seqs, members,
    )
    attention_cotangent, output_gradient, decoder_gradient = finish(
        middle, joint, rows, decoder_weight, decoder_sum,
        1.0 / math.sqrt(members * tok_rows * seqs), 1.0 / math.sqrt(members * grid_rows * seqs),
    )
    return (attention_cotangent[None], output_gradient, decoder_gradient)


def solution(mesh):
    in_specs = (
        P(("group", "member"), "seq", None),
        P(),
        P(),
        P(),
        P("seq", None),
        P(("group", "seq"), None),
        P("seq"),
    )
    out_specs = (P(("group", "member"), "seq", None), P(("group", "seq"), None), P("group", None))
    return jax.shard_map(body, mesh=mesh, in_specs=in_specs, out_specs=out_specs, check_vma=False)
```

```python
import functools
import math

import jax
import jax.numpy as jnp
from jax import lax
from jax.experimental import pallas as pl
from jax.experimental.pallas import tpu as pltpu
from jax.sharding import PartitionSpec as P

HEAD_DIM = 64
WINDOW = 512
REACH = 128
LANES = 128
COLS = 512

smooth = 0.1
f32 = jnp.float32
bf16 = jnp.bfloat16


def normalize(rows):
    values = rows.astype(f32)
    centre = jnp.mean(values, axis=-1, keepdims=True)
    values = values - centre
    spread = jnp.mean(values * values, axis=-1, keepdims=True)
    return (values * lax.rsqrt(spread + 1e-05)).astype(bf16)


def place_columns(mixed, scale):
    side = 256
    down = lax.broadcasted_iota(jnp.int32, (side, side), 0) >> 6
    across = lax.broadcasted_iota(jnp.int32, (side, side), 1) >> 6
    same = jnp.where(down == across, 1.0 / HEAD_DIM, 0.0).astype(bf16)
    pieces = []
    for at in range(0, mixed.shape[1], side):
        piece = mixed[:, at : at + side]
        mean = jnp.dot((piece * piece).astype(bf16), same, preferred_element_type=f32)
        pieces.append((piece * (lax.rsqrt(mean + 1e-06) * scale)).astype(bf16))
    return jnp.concatenate(pieces, axis=1)


def project(normed, weight, out, first, waits):
    width = weight.shape[0]
    for at in range(first, weight.shape[1], COLS):
        if waits:
            waits[at // COLS].wait()
        mixed = jnp.dot(normed[...], weight[:, at : at + COLS], preferred_element_type=f32)
        if at < 2 * width:
            mixed = place_columns(mixed, HEAD_DIM**-0.5 if at < width else 1.0)
        out[:, at - first : at - first + COLS] = mixed.astype(bf16)


def lane_block(j):
    return pl.ds(pl.multiple_of(j * LANES, LANES), LANES)


def low_lanes():
    return lax.broadcasted_iota(jnp.int32, (1, LANES), 1) < HEAD_DIM


def one_head(pair, head):
    return jnp.where(low_lanes() == (head == 0), pair, jnp.zeros_like(pair))


def with_counts(pair, head, real):
    ones = jnp.full(pair.shape, real, f32).astype(bf16)
    first = low_lanes()
    return jnp.where(first, pair, ones) if head == 0 else jnp.where(first, ones, pair)


def score(query, keys):
    return lax.dot_general(query, keys, (((1,), (1,)), ((), ())), preferred_element_type=f32)


def window_corner(scores, upper):
    rows = scores.shape[0] // 2
    down = lax.broadcasted_iota(jnp.int32, (rows, rows), 0)
    across = lax.broadcasted_iota(jnp.int32, (rows, rows), 1)
    late = across >= down
    blank = jnp.zeros((rows, rows), bf16)

    def corner(piece):
        weights = jnp.exp(piece)
        return (jnp.where(late, weights, 0.0) if upper else jnp.where(late, 0.0, weights)).astype(bf16)

    ends = (corner(scores[:rows, :rows]), corner(scores[rows:, rows:]))
    if upper:
        rest = jnp.exp(scores[:rows, rows:]).astype(bf16)
        lines = [[ends[0], rest], [blank, ends[1]]]
    else:
        rest = jnp.exp(scores[rows:, :rows]).astype(bf16)
        lines = [[ends[0], blank], [rest, ends[1]]]
    return jnp.concatenate([jnp.concatenate(line, axis=1) for line in lines], axis=0)


def attend_own(j, own, partial):
    rows, width = own.shape[0], own.shape[1] // 3
    half = rows // 2
    query = own[:, lane_block(j)]
    keys = own[:, lane_block(j + width // LANES)]
    values = own[:, lane_block(j + 2 * (width // LANES))]
    for head in range(2):
        scores = score(one_head(query, head), keys)
        early = [
            jnp.exp(scores[:half, :half]).astype(bf16), window_corner(scores[:half, half:], False),
        ]
        later = [
            window_corner(scores[half:, :half], True), jnp.exp(scores[half:, half:]).astype(bf16),
        ]
        weights = jnp.concatenate(
            [jnp.concatenate(early, axis=1), jnp.concatenate(later, axis=1)], axis=0
        )
        partial[2 * j + head] = jnp.dot(
            weights, with_counts(values, head, 1.0), preferred_element_type=f32
        )


def attend_beside(j, index, own, side, partial, attended, there):
    width = attended.shape[1]
    half = own.shape[0] // 2
    rows = slice(index * half, (index + 1) * half)
    query = own[rows, lane_block(j)]
    keys = side[rows, lane_block(j)]
    values = side[rows, lane_block(j + width // LANES)]
    totals = []
    for head in range(2):
        weights = window_corner(score(one_head(query, head), keys), index == 0)
        totals.append(
            jnp.dot(weights, with_counts(values, head, there), preferred_element_type=f32)
            + partial[2 * j + head, rows, :]
        )
    first = low_lanes()
    above = jnp.where(first, totals[0], totals[1])
    below = jnp.where(
        first, pltpu.roll(totals[0], HEAD_DIM, 1), pltpu.roll(totals[1], HEAD_DIM, 1)
    )
    attended[rows, lane_block(j)] = (above / below).astype(bf16)


def slope(diff):
    return diff * lax.rsqrt(diff * diff + smooth * smooth)


def copy_to(source, target, send, arrive, seq, member):
    return pltpu.make_async_remote_copy(
        src_ref=source,
        dst_ref=target,
        send_sem=send,
        recv_sem=arrive,
        device_id={"seq": seq, "member": member},
        device_id_type=pl.DeviceIdType.MESH,
    )


def layer_kernel(
    seqs, members, decoder, neighbours, area, tokens_far, weight_far, observed_far, output_far,
    middle_out, rows_out, decoder_out, joint,
    every, counts, turned, middle, edges, edges_in, terms, terms_in, pair, pair_in,
    sums, sums_in, mine,
    gathered_rows, gathered, tokens, attended, observed, output_weight,
    weight, normed, beside, own_parts, side_parts, mapped, partial, seen,
    attended_turned, tokens_turned, output_turned,
    halo_send, halo_in,
    local_sem, rim_send, rim_in, field_send, field_in, side_send, side_in, edge_send, edge_in, core_send, core_in,
    term_send, term_in,
    sum_send, sum_in, row_send, row_in, all_send, all_in,
):
    s, m = lax.axis_index("seq"), lax.axis_index("member")
    peers = seqs * members
    me = s * members + m
    ranks, x, c = members // 2, m // 2, lax.rem(m, 2)
    sibling = m + 1 - 2 * c
    tok_rows, fields = mapped.shape
    fan, grid_rows = neighbours.shape
    wide = tok_rows + 2 * REACH
    width = tokens.shape[1]
    chunk = width // peers

    def peer(step):
        flat = lax.rem(me + step, peers)
        return flat // members, lax.rem(flat, members)

    barrier = pltpu.get_barrier_semaphore()

    @pl.loop(1, peers)
    def _(step):
        seq, member = peer(step)
        pl.semaphore_signal(
            barrier, inc=1, device_id={"seq": seq, "member": member},
            device_id_type=pl.DeviceIdType.MESH,
        )

    columns = weight.shape[1] // COLS
    loads = [
        pltpu.make_async_copy(far, near, local_sem.at[i])
        for i, (far, near) in enumerate(
            [(tokens_far, tokens)]
            + [
                (weight_far.at[:, pl.ds(i * COLS, COLS)], weight.at[:, pl.ds(i * COLS, COLS)])
                for i in range(columns)
            ]
            + [(output_far, output_weight), (observed_far, observed)]
        )
    ]
    for load in loads:
        load.start()
    has_left, has_right = s > 0, s < seqs - 1
    half = WINDOW // 2

    def halo_copy(to_right):
        start, land, seq = (tok_rows - half, 0, s + 1) if to_right else (0, half, s - 1)
        return copy_to(
            tokens_far.at[pl.ds(start, half), :], beside.at[pl.ds(land, half), :],
            halo_send.at[to_right], halo_in.at[to_right], seq, m,
        )

    @pl.when(jnp.logical_not(has_left))
    def _():
        beside[:half, :] = jnp.zeros((half, width), bf16)

    @pl.when(jnp.logical_not(has_right))
    def _():
        beside[half:, :] = jnp.zeros((half, width), bf16)

    pl.semaphore_wait(barrier, peers - 1)

    @pl.when(has_right)
    def _():
        halo_copy(1).start()

    @pl.when(has_left)
    def _():
        halo_copy(0).start()

    loads[0].wait()
    normed[...] = normalize(tokens[...])
    project(normed, weight, own_parts, 0, loads[1 : 1 + columns])
    loads[1 + columns].wait()
    joint[...] = jnp.dot(
        output_weight[...], decoder[...], preferred_element_type=f32
    ).astype(bf16)
    mapped[...] = jnp.dot(tokens[...], decoder[...], preferred_element_type=f32)
    base = s * tok_rows - REACH
    block = 128
    loads[2 + columns].wait()

    @pl.loop(0, grid_rows // block)
    def _(i):
        cells = pl.ds(pl.multiple_of(i * block, block), block)
        local = neighbours[:, cells] - base
        place = lax.broadcasted_iota(jnp.int32, (wide, block), 0)
        total = jnp.zeros((wide, block), f32)
        for k in range(fan):
            total += jnp.where(local[k : k + 1, :] == place, 1.0 / fan, 0.0)
        counts[:, cells] = total.astype(bf16)
        seen[:, cells] = observed[cells, :].T

    blocks = width // LANES
    group = math.gcd(blocks, 4)

    @pl.loop(0, blocks // group)
    def _(i):
        for k in range(group):
            attend_own(i * group + k, own_parts, partial)

    @pl.when(has_left)
    def _():
        halo_copy(0).wait_send()
        halo_copy(1).wait_recv()

    @pl.when(has_right)
    def _():
        halo_copy(1).wait_send()
        halo_copy(0).wait_recv()

    normed[...] = normalize(beside[...])
    project(normed, weight, side_parts, width, None)
    bands = (
        (REACH, half), (REACH + half, half), (0, REACH), (REACH + tok_rows, REACH),
    )

    def field_copy(core, band, step):
        start, size = bands[band]
        cells = pl.ds(start, size)
        here = step if core else 0
        there = ranks * core + step
        member = sibling if core else 2 * lax.rem(x + step, ranks) + c
        return copy_to(
            every.at[pl.ds(here * fields, fields), cells],
            every.at[pl.ds(there * fields, fields), cells],
            field_send.at[band, there], field_in.at[band, there], s, member,
        )

    def side_copy(side):
        start, land, seq = ((tok_rows, 0, s + 1), (REACH, REACH + tok_rows, s - 1))[side]
        return copy_to(
            every.at[pl.ds(0, fields), pl.ds(start, REACH)],
            every.at[pl.ds(0, fields), pl.ds(land, REACH)],
            side_send.at[side], side_in.at[side], seq, m,
        )

    def rim_copy(side):
        start, land, seq = ((tok_rows, 0, s + 1), (REACH, REACH + tok_rows, s - 1))[side]
        return copy_to(
            attended_turned.at[:, pl.ds(start, REACH)],
            attended_turned.at[:, pl.ds(land, REACH)],
            rim_send.at[side], rim_in.at[side], seq, m,
        )

    def share(band):
        for step in range(1, ranks):
            field_copy(0, band, step).start()
        field_copy(1, band, 0).start()

    def forward(band):
        for step in range(1, ranks):
            field_copy(0, band, step).wait_recv()
            field_copy(1, band, step).start()

    def settle(band):
        for step in range(1, ranks):
            field_copy(0, band, step).wait_send()
        for step in range(ranks):
            field_copy(1, band, step).wait()

    for index in range(2):
        there = jnp.where((has_left, has_right)[index], 1.0, 0.0).astype(f32)
        for j in range(blocks):
            attend_beside(j, index, own_parts, side_parts, partial, attended, there)
        at = index * half
        total = mapped[at : at + half, :] + jnp.dot(
            attended[at : at + half, :], joint[...], preferred_element_type=f32
        )
        every[:fields, REACH + at : REACH + at + half] = total.T.astype(bf16)
        share(index)

        @pl.when((has_left, has_right)[index])
        def _():
            side_copy(1 - index).start()

        attended_turned[:, REACH + at : REACH + at + half] = attended[at : at + half, :].T

        @pl.when((has_left, has_right)[index])
        def _():
            rim_copy(1 - index).start()

    @pl.when(jnp.logical_not(has_left))
    def _():
        every[:, :REACH] = jnp.zeros((members * fields, REACH), bf16)
        attended_turned[:, :REACH] = jnp.zeros((width, REACH), bf16)
        edges_in[0] = jnp.zeros((REACH, fields), bf16)

    @pl.when(jnp.logical_not(has_right))
    def _():
        every[:, wide - REACH :] = jnp.zeros((members * fields, REACH), bf16)
        attended_turned[:, wide - REACH :] = jnp.zeros((width, REACH), bf16)
        edges_in[1] = jnp.zeros((REACH, fields), bf16)

    @pl.when(has_right)
    def _():
        side_copy(1).wait_recv()
        share(3)

    forward(0)
    tokens_turned[:, :REACH] = beside[half - REACH : half, :].T
    tokens_turned[:, REACH : REACH + tok_rows] = tokens[...].T
    tokens_turned[:, REACH + tok_rows :] = beside[half : half + REACH, :].T

    @pl.when(has_left)
    def _():
        side_copy(0).wait_recv()
        share(2)

    forward(1)
    output_turned[...] = output_weight[...].T

    @pl.when(has_right)
    def _():
        forward(3)
        side_copy(0).wait_send()

    @pl.when(has_left)
    def _():
        forward(2)
        side_copy(1).wait_send()

    settle(0)
    settle(1)

    @pl.when(has_right)
    def _():
        settle(3)

    @pl.when(has_left)
    def _():
        settle(2)

    block = math.gcd(grid_rows, 256)
    for at in range(0, grid_rows, block):
        cells = slice(at, at + block)
        found = jnp.dot(every[...], counts[:, cells], preferred_element_type=f32)
        mean = found[:fields, :]
        pairs = jnp.zeros((fields, block), f32)
        for step in range(1, members):
            pairs += slope(mean - found[step * fields : (step + 1) * fields, :])
        single = slope(mean - seen[:, cells])
        turned[:, cells] = (
            area[:, cells]
            * (single * (1.0 / members) - pairs * (1.0 / (members * (members - 1))))
        ).astype(bf16)

    def spread(places):
        return score(places, turned[...])

    reached = spread(counts[...])
    rounded = reached.astype(bf16)
    edges[0] = rounded[:REACH]
    edges[1] = rounded[wide - REACH :]

    def edge_copy(side):
        return copy_to(
            edges.at[side], edges_in.at[1 - side], edge_send.at[side], edge_in.at[side],
            s - 1 if side == 0 else s + 1, m,
        )

    @pl.when(has_left)
    def _():
        edge_copy(0).start()

    @pl.when(has_right)
    def _():
        edge_copy(1).start()

    middle[...] = reached[REACH : wide - REACH]

    @pl.when(has_left)
    def _():
        rim_copy(1).wait_send()
        rim_copy(0).wait_recv()

    @pl.when(has_right)
    def _():
        rim_copy(0).wait_send()
        rim_copy(1).wait_recv()

    output_term = jnp.dot(attended_turned[...], rounded, preferred_element_type=f32)
    spots = seqs * ranks
    spot = s * ranks + x

    def put(part, value):
        rows = value.astype(bf16)
        for core in range(2):
            for rank in range(ranks):
                for seq in range(seqs):
                    at = (seq * members + 2 * rank + core) * chunk
                    terms[part, core, rank, seq] = rows[at : at + chunk, :]

    def core_copy(part):
        return copy_to(
            terms.at[part, 1 - c], terms_in.at[part], core_send.at[part], core_in.at[part],
            s, sibling,
        )

    def rank_copy(part, step):
        rank = lax.rem(x + step, ranks)
        return copy_to(
            pair.at[part, rank], pair_in.at[part, step],
            term_send.at[part, step], term_in.at[part, step], s, 2 * rank + c,
        )

    def sum_copy(part, step):
        seq = lax.rem(s + step, seqs)
        return copy_to(
            sums.at[part, seq], sums_in.at[part, step],
            sum_send.at[part, step], sum_in.at[part, step], seq, m,
        )

    def row_copy(step):
        return copy_to(
            mine.at[0], gathered_rows.at[m], row_send.at[step], row_in.at[step],
            s, lax.rem(m + step, members),
        )

    def all_copy(step):
        other = lax.rem(spot + step, spots)
        return copy_to(
            mine.at[1], gathered.at[c, spot], all_send.at[step], all_in.at[step],
            other // ranks, 2 * lax.rem(other, ranks) + c,
        )

    def last_copy():
        return copy_to(
            gathered.at[c], gathered.at[c], core_send.at[2], core_in.at[2], s, sibling
        )

    def add_cores(part):
        core_copy(part).wait()
        pair[part] = (terms[part, c].astype(f32) + terms_in[part].astype(f32)).astype(bf16)
        for step in range(1, ranks):
            rank_copy(part, step).start()

    def add_ranks(part):
        for step in range(1, ranks):
            rank_copy(part, step).wait()
        total = pair[part, x].astype(f32)
        for step in range(1, ranks):
            total += pair_in[part, step].astype(f32)
        sums[part] = total.astype(bf16)

        @pl.loop(1, seqs)
        def _(step):
            sum_copy(part, step).start()

    def add_seqs(part):
        @pl.loop(1, seqs)
        def _(step):
            sum_copy(part, step).wait()

        total = sums[part, s].astype(f32)
        for step in range(1, seqs):
            total += sums_in[part, step].astype(f32)
        mine[part] = total.astype(bf16)

    put(0, output_term)
    core_copy(0).start()
    decoder_term = jnp.dot(tokens_turned[...], rounded, preferred_element_type=f32)
    add_cores(0)
    decoder_term += jnp.dot(
        output_turned[...], output_term.astype(bf16), preferred_element_type=f32
    )
    put(1, decoder_term)
    core_copy(1).start()
    add_cores(1)

    @pl.when(has_left)
    def _():
        edge_copy(0).wait_send()
        edge_copy(1).wait_recv()

    @pl.when(has_right)
    def _():
        edge_copy(1).wait_send()
        edge_copy(0).wait_recv()

    middle[:REACH, :] += edges_in[0].astype(f32)
    middle[tok_rows - REACH :, :] += edges_in[1].astype(f32)
    middle_out[...] = middle[...].astype(bf16)
    add_ranks(0)
    add_ranks(1)
    add_seqs(0)
    for step in range(1, members):
        row_copy(step).start()
    gathered_rows[m] = mine[0]
    add_seqs(1)

    @pl.loop(1, spots)
    def _(step):
        all_copy(step).start()

    gathered[c, spot] = mine[1]
    for step in range(1, members):
        row_copy(step).wait()
    rows_out[...] = gathered_rows[...]

    @pl.loop(1, spots)
    def _(step):
        all_copy(step).wait()

    last_copy().start()
    last_copy().wait()
    decoder_out[...] = gathered[...]


def layer(decoder, neighbours, area, tokens, weight, observed, output_weight, seqs, members):
    tok_rows, width = tokens.shape
    fields = decoder.shape[1]
    grid_rows = neighbours.shape[1]
    wide = tok_rows + 2 * REACH
    ranks = members // 2
    chunk = width // (seqs * members)
    near = pl.BlockSpec(memory_space=pltpu.VMEM)
    far = pl.BlockSpec(memory_space=pl.ANY)
    dma = pltpu.SemaphoreType.DMA
    return pl.pallas_call(
        functools.partial(layer_kernel, seqs, members),
        in_specs=[near] * 3 + [far] * 4,
        out_specs=[near] * 4,
        out_shape=[
            pltpu.VMEM((tok_rows, fields), bf16),
            pltpu.VMEM((members, chunk, fields), bf16),
            pltpu.VMEM((2, seqs * ranks, chunk, fields), bf16),
            pltpu.VMEM((width, fields), bf16),
        ],
        scratch_shapes=[
            pltpu.VMEM((members * fields, wide), bf16),
            pltpu.VMEM((wide, grid_rows), bf16),
            pltpu.VMEM((fields, grid_rows), bf16),
            pltpu.VMEM((tok_rows, fields), f32),
            pltpu.VMEM((2, REACH, fields), bf16),
            pltpu.VMEM((2, REACH, fields), bf16),
            pltpu.VMEM((2, 2, ranks, seqs, chunk, fields), bf16),
            pltpu.VMEM((2, ranks, seqs, chunk, fields), bf16),
            pltpu.VMEM((2, ranks, seqs, chunk, fields), bf16),
            pltpu.VMEM((2, ranks, seqs, chunk, fields), bf16),
            pltpu.VMEM((2, seqs, chunk, fields), bf16),
            pltpu.VMEM((2, seqs, chunk, fields), bf16),
            pltpu.VMEM((2, chunk, fields), bf16),
            pltpu.VMEM((members, chunk, fields), bf16),
            pltpu.VMEM((2, seqs * ranks, chunk, fields), bf16),
            pltpu.VMEM(tokens.shape, bf16),
            pltpu.VMEM(tokens.shape, bf16),
            pltpu.VMEM(observed.shape, f32),
            pltpu.VMEM(output_weight.shape, bf16),
            pltpu.VMEM(weight.shape, bf16),
            pltpu.VMEM(tokens.shape, bf16),
            pltpu.VMEM((WINDOW, width), bf16),
            pltpu.VMEM((tok_rows, 3 * width), bf16),
            pltpu.VMEM((WINDOW, 2 * width), bf16),
            pltpu.VMEM((tok_rows, fields), f32),
            pltpu.VMEM((2 * (width // LANES), tok_rows, LANES), f32),
            pltpu.VMEM((fields, grid_rows), f32),
            pltpu.VMEM((width, wide), bf16),
            pltpu.VMEM((width, wide), bf16),
            pltpu.VMEM((width, width), bf16),
            dma((2,)),
            dma((2,)),
            dma((3 + weight.shape[1] // COLS,)),
            dma((2,)),
            dma((2,)),
            dma((4, members)),
            dma((4, members)),
            dma((2,)),
            dma((2,)),
            dma((2,)),
            dma((2,)),
            dma((3,)),
            dma((3,)),
            dma((2, ranks)),
            dma((2, ranks)),
            dma((2, seqs)),
            dma((2, seqs)),
            dma((members,)),
            dma((members,)),
            dma((seqs * ranks,)),
            dma((seqs * ranks,)),
        ],
        compiler_params=pltpu.CompilerParams(
            vmem_limit_bytes=56 << 20, collective_id=0, has_side_effects=True
        ),
    )(decoder, neighbours, area, tokens, weight, observed, output_weight)


def finish_kernel(
    output_scale, decoder_scale, middle, joint, rows, decoder, decoder_sum,
    cotangent_far, output_far, decoder_far, cotangent, output, decoder_near, sems,
):
    copies = []

    def send(near, far, part):
        copy = pltpu.make_async_copy(near.at[part], far.at[part], sems.at[len(copies)])
        copy.start()
        copies.append(copy)

    cores, spots, chunk, _ = decoder_sum.shape
    for spot in range(spots):
        for core in range(cores):
            at = (cores * spot + core) * chunk
            decoder_near[at : at + chunk, :] = decoder_sum[core, spot].astype(f32) * decoder_scale
    send(decoder_near, decoder_far, slice(None))
    output[...] = score(rows[...].reshape(output.shape[0], -1), decoder[...]) * output_scale
    send(output, output_far, slice(None))
    size = cotangent.shape[0] // 2
    for part in range(2):
        at = slice(part * size, (part + 1) * size)
        cotangent[at, :] = score(middle[at, :], joint[...]).astype(bf16)
        send(cotangent, cotangent_far, pl.ds(part * size, size))
    for copy in copies:
        copy.wait()


def finish(middle, joint, rows, decoder, decoder_sum, output_scale, decoder_scale):
    width, fields = decoder.shape
    shapes = [
        jax.ShapeDtypeStruct((middle.shape[0], width), bf16),
        jax.ShapeDtypeStruct((rows.shape[0] * rows.shape[1], width), f32),
        jax.ShapeDtypeStruct((width, fields), f32),
    ]
    return pl.pallas_call(
        functools.partial(finish_kernel, output_scale, decoder_scale),
        in_specs=[pl.BlockSpec(memory_space=pltpu.VMEM)] * 5,
        out_specs=[pl.BlockSpec(memory_space=pl.ANY)] * 3,
        out_shape=shapes,
        scratch_shapes=[pltpu.VMEM(shape.shape, shape.dtype) for shape in shapes]
        + [pltpu.SemaphoreType.DMA((4,))],
        compiler_params=pltpu.CompilerParams(vmem_limit_bytes=16 << 20),
    )(middle, joint, rows, decoder, decoder_sum)


def body(tokens, input_weight, output_weight, decoder_weight, neighbours, observed, cell_area):
    own_tokens = tokens[0]
    tok_rows, width = own_tokens.shape
    fields = decoder_weight.shape[1]
    seqs = lax.axis_size("seq")
    members = lax.axis_size("member")
    grid_rows = neighbours.shape[0]
    middle, rows, decoder_sum, joint = layer(
        decoder_weight, neighbours.T, cell_area[None, :], own_tokens, input_weight, observed,
        output_weight, seqs, members,
    )
    attention_cotangent, output_gradient, decoder_gradient = finish(
        middle, joint, rows, decoder_weight, decoder_sum,
        1.0 / math.sqrt(members * tok_rows * seqs), 1.0 / math.sqrt(members * grid_rows * seqs),
    )
    return (attention_cotangent[None], output_gradient, decoder_gradient)


def solution(mesh):
    in_specs = (
        P(("group", "member"), "seq", None),
        P(),
        P(),
        P(),
        P("seq", None),
        P(("group", "seq"), None),
        P("seq"),
    )
    out_specs = (P(("group", "member"), "seq", None), P(("group", "seq"), None), P("group", None))
    return jax.shard_map(body, mesh=mesh, in_specs=in_specs, out_specs=out_specs, check_vma=False)
```

```python
import functools
import math

import jax
import jax.numpy as jnp
from jax import lax
from jax.experimental import pallas as pl
from jax.experimental.pallas import tpu as pltpu
from jax.sharding import PartitionSpec as P

HEAD_DIM = 64
WINDOW = 512
REACH = 128
LANES = 128
COLS = 512

smooth = 0.1
f32 = jnp.float32
bf16 = jnp.bfloat16


def normalize(rows):
    values = rows.astype(f32)
    centre = jnp.mean(values, axis=-1, keepdims=True)
    values = values - centre
    spread = jnp.mean(values * values, axis=-1, keepdims=True)
    return (values * lax.rsqrt(spread + 1e-05)).astype(bf16)


def place_columns(mixed, scale):
    side = 256
    down = lax.broadcasted_iota(jnp.int32, (side, side), 0) >> 6
    across = lax.broadcasted_iota(jnp.int32, (side, side), 1) >> 6
    same = jnp.where(down == across, 1.0 / HEAD_DIM, 0.0).astype(bf16)
    pieces = []
    for at in range(0, mixed.shape[1], side):
        piece = mixed[:, at : at + side]
        mean = jnp.dot((piece * piece).astype(bf16), same, preferred_element_type=f32)
        pieces.append((piece * (lax.rsqrt(mean + 1e-06) * scale)).astype(bf16))
    return jnp.concatenate(pieces, axis=1)


def project(normed, weight, out, first, waits):
    width = weight.shape[0]
    for at in range(first, weight.shape[1], COLS):
        if waits:
            waits[at // COLS].wait()
        mixed = jnp.dot(normed[...], weight[:, at : at + COLS], preferred_element_type=f32)
        if at < 2 * width:
            mixed = place_columns(mixed, HEAD_DIM**-0.5 if at < width else 1.0)
        out[:, at - first : at - first + COLS] = mixed.astype(bf16)


def lane_block(j):
    return pl.ds(pl.multiple_of(j * LANES, LANES), LANES)


def low_lanes():
    return lax.broadcasted_iota(jnp.int32, (1, LANES), 1) < HEAD_DIM


def one_head(pair, head):
    return jnp.where(low_lanes() == (head == 0), pair, jnp.zeros_like(pair))


def with_counts(pair, head, real):
    ones = jnp.full(pair.shape, real, f32).astype(bf16)
    first = low_lanes()
    return jnp.where(first, pair, ones) if head == 0 else jnp.where(first, ones, pair)


def score(query, keys):
    return lax.dot_general(query, keys, (((1,), (1,)), ((), ())), preferred_element_type=f32)


def window_corner(scores, upper):
    rows = scores.shape[0] // 2
    down = lax.broadcasted_iota(jnp.int32, (rows, rows), 0)
    across = lax.broadcasted_iota(jnp.int32, (rows, rows), 1)
    late = across >= down
    blank = jnp.zeros((rows, rows), bf16)

    def corner(piece):
        weights = jnp.exp(piece)
        return (jnp.where(late, weights, 0.0) if upper else jnp.where(late, 0.0, weights)).astype(bf16)

    ends = (corner(scores[:rows, :rows]), corner(scores[rows:, rows:]))
    if upper:
        rest = jnp.exp(scores[:rows, rows:]).astype(bf16)
        lines = [[ends[0], rest], [blank, ends[1]]]
    else:
        rest = jnp.exp(scores[rows:, :rows]).astype(bf16)
        lines = [[ends[0], blank], [rest, ends[1]]]
    return jnp.concatenate([jnp.concatenate(line, axis=1) for line in lines], axis=0)


def attend_own(j, own, partial):
    rows, width = own.shape[0], own.shape[1] // 3
    half = rows // 2
    query = own[:, lane_block(j)]
    keys = own[:, lane_block(j + width // LANES)]
    values = own[:, lane_block(j + 2 * (width // LANES))]
    for head in range(2):
        scores = score(one_head(query, head), keys)
        early = [
            jnp.exp(scores[:half, :half]).astype(bf16), window_corner(scores[:half, half:], False),
        ]
        later = [
            window_corner(scores[half:, :half], True), jnp.exp(scores[half:, half:]).astype(bf16),
        ]
        weights = jnp.concatenate(
            [jnp.concatenate(early, axis=1), jnp.concatenate(later, axis=1)], axis=0
        )
        partial[2 * j + head] = jnp.dot(
            weights, with_counts(values, head, 1.0), preferred_element_type=f32
        )


def attend_beside(j, index, own, side, partial, attended, there):
    width = attended.shape[1]
    half = own.shape[0] // 2
    rows = slice(index * half, (index + 1) * half)
    query = own[rows, lane_block(j)]
    keys = side[rows, lane_block(j)]
    values = side[rows, lane_block(j + width // LANES)]
    totals = []
    for head in range(2):
        weights = window_corner(score(one_head(query, head), keys), index == 0)
        totals.append(
            jnp.dot(weights, with_counts(values, head, there), preferred_element_type=f32)
            + partial[2 * j + head, rows, :]
        )
    first = low_lanes()
    above = jnp.where(first, totals[0], totals[1])
    below = jnp.where(
        first, pltpu.roll(totals[0], HEAD_DIM, 1), pltpu.roll(totals[1], HEAD_DIM, 1)
    )
    attended[rows, lane_block(j)] = (above / below).astype(bf16)


def slope(diff):
    return diff * lax.rsqrt(diff * diff + smooth * smooth)


def copy_to(source, target, send, arrive, seq, member):
    return pltpu.make_async_remote_copy(
        src_ref=source,
        dst_ref=target,
        send_sem=send,
        recv_sem=arrive,
        device_id={"seq": seq, "member": member},
        device_id_type=pl.DeviceIdType.MESH,
    )


def layer_kernel(
    seqs, members, decoder, neighbours, area, tokens_far, weight_far, observed_far, output_far,
    middle_out, rows_out, decoder_out, joint,
    every, counts, turned, middle, edges, edges_in, terms, terms_in, pair, pair_in,
    sums, sums_in, mine,
    gathered_rows, gathered, tokens, attended, observed, output_weight,
    weight, normed, beside, own_parts, side_parts, mapped, partial, seen,
    attended_turned, latent_turned, pooled,
    halo_send, halo_in, met,
    local_sem, rim_send, rim_in, field_send, field_in, side_send, side_in, edge_send, edge_in, core_send, core_in,
    term_send, term_in,
    sum_send, sum_in, row_send, row_in, all_send, all_in,
):
    s, m = lax.axis_index("seq"), lax.axis_index("member")
    peers = seqs * members
    ranks, x, c = members // 2, m // 2, lax.rem(m, 2)
    sibling = m + 1 - 2 * c
    tok_rows, fields = mapped.shape
    fan, grid_rows = neighbours.shape
    wide = tok_rows + 2 * REACH
    width = tokens.shape[1]
    chunk = width // peers

    barrier = pltpu.get_barrier_semaphore()

    def tell(semaphore, seq, member):
        pl.semaphore_signal(
            semaphore, inc=1, device_id={"seq": seq, "member": member},
            device_id_type=pl.DeviceIdType.MESH,
        )

    has_left, has_right = s > 0, s < seqs - 1

    @pl.when(has_left)
    def _():
        tell(barrier, s - 1, m)

    @pl.when(has_right)
    def _():
        tell(barrier, s + 1, m)

    for step in range(1, members):
        tell(barrier, s, lax.rem(m + step, members))

    columns = weight.shape[1] // COLS
    loads = [
        pltpu.make_async_copy(far, near, local_sem.at[i])
        for i, (far, near) in enumerate(
            [(tokens_far, tokens)]
            + [
                (weight_far.at[:, pl.ds(i * COLS, COLS)], weight.at[:, pl.ds(i * COLS, COLS)])
                for i in range(columns)
            ]
            + [(output_far, output_weight), (observed_far, observed)]
        )
    ]
    for load in loads:
        load.start()
    half = WINDOW // 2

    def halo_copy(to_right):
        start, land, seq = (tok_rows - half, 0, s + 1) if to_right else (0, half, s - 1)
        return copy_to(
            tokens_far.at[pl.ds(start, half), :], beside.at[pl.ds(land, half), :],
            halo_send.at[to_right], halo_in.at[to_right], seq, m,
        )

    @pl.when(jnp.logical_not(has_left))
    def _():
        beside[:half, :] = jnp.zeros((half, width), bf16)

    @pl.when(jnp.logical_not(has_right))
    def _():
        beside[half:, :] = jnp.zeros((half, width), bf16)

    near = members - 1 + jnp.minimum(s, 1) + jnp.minimum(seqs - 1 - s, 1)
    pl.semaphore_wait(barrier, near)

    @pl.when(has_right)
    def _():
        halo_copy(1).start()

    @pl.when(has_left)
    def _():
        halo_copy(0).start()

    loads[0].wait()
    normed[...] = normalize(tokens[...])
    project(normed, weight, own_parts, 0, loads[1 : 1 + columns])
    loads[1 + columns].wait()
    joint[...] = jnp.dot(
        output_weight[...], decoder[...], preferred_element_type=f32
    ).astype(bf16)
    mapped[...] = jnp.dot(tokens[...], decoder[...], preferred_element_type=f32)
    base = s * tok_rows - REACH
    block = 128
    loads[2 + columns].wait()

    @pl.loop(0, grid_rows // block)
    def _(i):
        cells = pl.ds(pl.multiple_of(i * block, block), block)
        local = neighbours[:, cells] - base
        place = lax.broadcasted_iota(jnp.int32, (wide, block), 0)
        total = jnp.zeros((wide, block), f32)
        for k in range(fan):
            total += jnp.where(local[k : k + 1, :] == place, 1.0 / fan, 0.0)
        counts[:, cells] = total.astype(bf16)
        seen[:, cells] = observed[cells, :].T

    blocks = width // LANES
    group = math.gcd(blocks, 4)

    @pl.loop(0, blocks // group)
    def _(i):
        for k in range(group):
            attend_own(i * group + k, own_parts, partial)

    @pl.when(has_left)
    def _():
        halo_copy(0).wait_send()
        halo_copy(1).wait_recv()

    @pl.when(has_right)
    def _():
        halo_copy(1).wait_send()
        halo_copy(0).wait_recv()

    def meet(round, receive):
        far = 2 << round

        @pl.when(s >= far)
        def _():
            if receive:
                pl.semaphore_wait(met.at[round, 0], 1)
            else:
                tell(met.at[round, 1], s - far, m)

        @pl.when(s + far < seqs)
        def _():
            if receive:
                pl.semaphore_wait(met.at[round, 1], 1)
            else:
                tell(met.at[round, 0], s + far, m)

    rounds = max(0, (seqs - 1).bit_length() - 1)
    if rounds:
        meet(0, False)
    normed[...] = normalize(beside[...])
    project(normed, weight, side_parts, width, None)
    bands = (
        (REACH, half), (REACH + half, half), (0, REACH), (REACH + tok_rows, REACH),
    )

    def field_copy(core, band, step):
        start, size = bands[band]
        cells = pl.ds(start, size)
        here = step if core else 0
        there = ranks * core + step
        member = sibling if core else 2 * lax.rem(x + step, ranks) + c
        return copy_to(
            every.at[pl.ds(here * fields, fields), cells],
            every.at[pl.ds(there * fields, fields), cells],
            field_send.at[band, there], field_in.at[band, there], s, member,
        )

    def side_copy(side):
        start, land, seq = ((tok_rows, 0, s + 1), (REACH, REACH + tok_rows, s - 1))[side]
        return copy_to(
            every.at[pl.ds(0, fields), pl.ds(start, REACH)],
            every.at[pl.ds(0, fields), pl.ds(land, REACH)],
            side_send.at[side], side_in.at[side], seq, m,
        )

    def rim_copy(side):
        start, land, seq = ((tok_rows, 0, s + 1), (REACH, REACH + tok_rows, s - 1))[side]
        return copy_to(
            latent_turned.at[:, pl.ds(start, REACH)],
            latent_turned.at[:, pl.ds(land, REACH)],
            rim_send.at[side], rim_in.at[side], seq, m,
        )

    def share(band):
        for step in range(1, ranks):
            field_copy(0, band, step).start()
        field_copy(1, band, 0).start()

    def forward(band):
        for step in range(1, ranks):
            field_copy(0, band, step).wait_recv()
            field_copy(1, band, step).start()

    def settle(band):
        for step in range(1, ranks):
            field_copy(0, band, step).wait_send()
        for step in range(ranks):
            field_copy(1, band, step).wait()

    for index in range(2):
        there = jnp.where((has_left, has_right)[index], 1.0, 0.0).astype(f32)
        for j in range(blocks):
            attend_beside(j, index, own_parts, side_parts, partial, attended, there)
        at = index * half
        total = mapped[at : at + half, :] + jnp.dot(
            attended[at : at + half, :], joint[...], preferred_element_type=f32
        )
        every[:fields, REACH + at : REACH + at + half] = total.T.astype(bf16)
        share(index)

        @pl.when((has_left, has_right)[index])
        def _():
            side_copy(1 - index).start()

    @pl.when(jnp.logical_not(has_left))
    def _():
        every[:, :REACH] = jnp.zeros((members * fields, REACH), bf16)
        latent_turned[:, :REACH] = jnp.zeros((width, REACH), bf16)
        edges_in[0] = jnp.zeros((REACH, fields), bf16)

    @pl.when(jnp.logical_not(has_right))
    def _():
        every[:, wide - REACH :] = jnp.zeros((members * fields, REACH), bf16)
        latent_turned[:, wide - REACH :] = jnp.zeros((width, REACH), bf16)
        edges_in[1] = jnp.zeros((REACH, fields), bf16)

    def settle_latent(index):
        rows = slice(index * half, (index + 1) * half)
        latent = tokens[rows, :].astype(f32) + jnp.dot(
            attended[rows, :], output_weight[...], preferred_element_type=f32
        )
        start = REACH + index * half
        latent_turned[:, start : start + half] = latent.astype(bf16).T

        @pl.when((has_left, has_right)[index])
        def _():
            rim_copy(1 - index).start()

    settle_latent(0)

    @pl.when(has_right)
    def _():
        side_copy(1).wait_recv()
        share(3)

    forward(0)
    settle_latent(1)

    @pl.when(has_left)
    def _():
        side_copy(0).wait_recv()
        share(2)

    attended_turned[...] = attended[...].T
    forward(1)

    @pl.when(has_right)
    def _():
        forward(3)
        side_copy(0).wait_send()

    @pl.when(has_left)
    def _():
        forward(2)
        side_copy(1).wait_send()

    settle(0)
    settle(1)
    block = math.gcd(grid_rows, 256)
    cuts = [slice(at, at + block) for at in range(0, grid_rows, block)]
    for cells in cuts:
        pooled[:, cells] = jnp.dot(
            every[:, REACH : wide - REACH], counts[REACH : wide - REACH, cells],
            preferred_element_type=f32,
        )

    @pl.when(has_right)
    def _():
        settle(3)

    @pl.when(has_left)
    def _():
        settle(2)

    outer = jnp.concatenate([every[:, :REACH], every[:, wide - REACH :]], axis=1)
    for cells in cuts:
        places = jnp.concatenate([counts[:REACH, cells], counts[wide - REACH :, cells]], axis=0)
        found = pooled[:, cells] + jnp.dot(outer, places, preferred_element_type=f32)
        mean = found[:fields, :]
        pairs = jnp.zeros((fields, block), f32)
        for step in range(1, members):
            pairs += slope(mean - found[step * fields : (step + 1) * fields, :])
        single = slope(mean - seen[:, cells])
        turned[:, cells] = (
            area[:, cells]
            * (single * (1.0 / members) - pairs * (1.0 / (members * (members - 1))))
        ).astype(bf16)

    def spread(places):
        return score(places, turned[...])

    reached = spread(counts[...])
    rounded = reached.astype(bf16)
    edges[0] = rounded[:REACH]
    edges[1] = rounded[wide - REACH :]

    def edge_copy(side):
        return copy_to(
            edges.at[side], edges_in.at[1 - side], edge_send.at[side], edge_in.at[side],
            s - 1 if side == 0 else s + 1, m,
        )

    @pl.when(has_left)
    def _():
        edge_copy(0).start()

    @pl.when(has_right)
    def _():
        edge_copy(1).start()

    middle[...] = reached[REACH : wide - REACH]

    @pl.when(has_left)
    def _():
        rim_copy(1).wait_send()
        rim_copy(0).wait_recv()

    @pl.when(has_right)
    def _():
        rim_copy(0).wait_send()
        rim_copy(1).wait_recv()

    for round in range(rounds):
        meet(round, True)
        if round + 1 < rounds:
            meet(round + 1, False)

    spots = seqs * ranks
    spot = s * ranks + x

    def put(part, value):
        rows = value.astype(bf16)
        for core in range(2):
            for rank in range(ranks):
                for seq in range(seqs):
                    at = (seq * members + 2 * rank + core) * chunk
                    terms[part, core, rank, seq] = rows[at : at + chunk, :]

    def core_copy(part):
        return copy_to(
            terms.at[part, 1 - c], terms_in.at[part], core_send.at[part], core_in.at[part],
            s, sibling,
        )

    def rank_copy(part, step):
        rank = lax.rem(x + step, ranks)
        return copy_to(
            pair.at[part, rank], pair_in.at[part, step],
            term_send.at[part, step], term_in.at[part, step], s, 2 * rank + c,
        )

    def sum_copy(part, step):
        seq = lax.rem(s + step, seqs)
        return copy_to(
            sums.at[part, seq], sums_in.at[part, step],
            sum_send.at[part, step], sum_in.at[part, step], seq, m,
        )

    def row_copy(step):
        return copy_to(
            mine.at[0], gathered_rows.at[m], row_send.at[step], row_in.at[step],
            s, lax.rem(m + step, members),
        )

    def all_copy(step):
        other = lax.rem(spot + step, spots)
        return copy_to(
            mine.at[1], gathered.at[c, spot], all_send.at[step], all_in.at[step],
            other // ranks, 2 * lax.rem(other, ranks) + c,
        )

    def last_copy():
        return copy_to(
            gathered.at[c], gathered.at[c], core_send.at[2], core_in.at[2], s, sibling
        )

    def add_cores(part):
        core_copy(part).wait()
        pair[part] = (terms[part, c].astype(f32) + terms_in[part].astype(f32)).astype(bf16)
        for step in range(1, ranks):
            rank_copy(part, step).start()

    def add_ranks(part):
        for step in range(1, ranks):
            rank_copy(part, step).wait()
        total = pair[part, x].astype(f32)
        for step in range(1, ranks):
            total += pair_in[part, step].astype(f32)
        sums[part] = total.astype(bf16)

        @pl.loop(1, seqs)
        def _(step):
            sum_copy(part, step).start()

    def add_seqs(part):
        @pl.loop(1, seqs)
        def _(step):
            sum_copy(part, step).wait()

        total = sums[part, s].astype(f32)
        for step in range(1, seqs):
            total += sums_in[part, step].astype(f32)
        mine[part] = total.astype(bf16)

    put(1, jnp.dot(latent_turned[...], rounded, preferred_element_type=f32))
    core_copy(1).start()
    add_cores(1)

    @pl.when(has_left)
    def _():
        edge_copy(0).wait_send()
        edge_copy(1).wait_recv()

    @pl.when(has_right)
    def _():
        edge_copy(1).wait_send()
        edge_copy(0).wait_recv()

    middle[:REACH, :] += edges_in[0].astype(f32)
    middle[tok_rows - REACH :, :] += edges_in[1].astype(f32)
    whole = middle[...].astype(bf16)
    middle_out[...] = whole
    put(0, jnp.dot(attended_turned[...], whole, preferred_element_type=f32))
    core_copy(0).start()
    add_cores(0)
    add_ranks(1)
    add_ranks(0)
    add_seqs(1)

    @pl.loop(1, spots)
    def _(step):
        all_copy(step).start()

    add_seqs(0)
    for step in range(1, members):
        row_copy(step).start()
    gathered_rows[m] = mine[0]
    gathered[c, spot] = mine[1]
    for step in range(1, members):
        row_copy(step).wait()
    rows_out[...] = gathered_rows[...]

    @pl.loop(1, spots)
    def _(step):
        all_copy(step).wait()

    last_copy().start()
    last_copy().wait()
    decoder_out[...] = gathered[...]


def layer(decoder, neighbours, area, tokens, weight, observed, output_weight, seqs, members):
    tok_rows, width = tokens.shape
    fields = decoder.shape[1]
    grid_rows = neighbours.shape[1]
    wide = tok_rows + 2 * REACH
    ranks = members // 2
    chunk = width // (seqs * members)
    near = pl.BlockSpec(memory_space=pltpu.VMEM)
    far = pl.BlockSpec(memory_space=pl.ANY)
    dma = pltpu.SemaphoreType.DMA
    return pl.pallas_call(
        functools.partial(layer_kernel, seqs, members),
        in_specs=[near] * 3 + [far] * 4,
        out_specs=[near] * 4,
        out_shape=[
            pltpu.VMEM((tok_rows, fields), bf16),
            pltpu.VMEM((members, chunk, fields), bf16),
            pltpu.VMEM((2, seqs * ranks, chunk, fields), bf16),
            pltpu.VMEM((width, fields), bf16),
        ],
        scratch_shapes=[
            pltpu.VMEM((members * fields, wide), bf16),
            pltpu.VMEM((wide, grid_rows), bf16),
            pltpu.VMEM((fields, grid_rows), bf16),
            pltpu.VMEM((tok_rows, fields), f32),
            pltpu.VMEM((2, REACH, fields), bf16),
            pltpu.VMEM((2, REACH, fields), bf16),
            pltpu.VMEM((2, 2, ranks, seqs, chunk, fields), bf16),
            pltpu.VMEM((2, ranks, seqs, chunk, fields), bf16),
            pltpu.VMEM((2, ranks, seqs, chunk, fields), bf16),
            pltpu.VMEM((2, ranks, seqs, chunk, fields), bf16),
            pltpu.VMEM((2, seqs, chunk, fields), bf16),
            pltpu.VMEM((2, seqs, chunk, fields), bf16),
            pltpu.VMEM((2, chunk, fields), bf16),
            pltpu.VMEM((members, chunk, fields), bf16),
            pltpu.VMEM((2, seqs * ranks, chunk, fields), bf16),
            pltpu.VMEM(tokens.shape, bf16),
            pltpu.VMEM(tokens.shape, bf16),
            pltpu.VMEM(observed.shape, f32),
            pltpu.VMEM(output_weight.shape, bf16),
            pltpu.VMEM(weight.shape, bf16),
            pltpu.VMEM(tokens.shape, bf16),
            pltpu.VMEM((WINDOW, width), bf16),
            pltpu.VMEM((tok_rows, 3 * width), bf16),
            pltpu.VMEM((WINDOW, 2 * width), bf16),
            pltpu.VMEM((tok_rows, fields), f32),
            pltpu.VMEM((2 * (width // LANES), tok_rows, LANES), f32),
            pltpu.VMEM((fields, grid_rows), f32),
            pltpu.VMEM((width, tok_rows), bf16),
            pltpu.VMEM((width, wide), bf16),
            pltpu.VMEM((members * fields, grid_rows), f32),
            dma((2,)),
            dma((2,)),
            pltpu.SemaphoreType.REGULAR((max(1, (seqs - 1).bit_length() - 1), 2)),
            dma((3 + weight.shape[1] // COLS,)),
            dma((2,)),
            dma((2,)),
            dma((4, members)),
            dma((4, members)),
            dma((2,)),
            dma((2,)),
            dma((2,)),
            dma((2,)),
            dma((3,)),
            dma((3,)),
            dma((2, ranks)),
            dma((2, ranks)),
            dma((2, seqs)),
            dma((2, seqs)),
            dma((members,)),
            dma((members,)),
            dma((seqs * ranks,)),
            dma((seqs * ranks,)),
        ],
        compiler_params=pltpu.CompilerParams(
            vmem_limit_bytes=56 << 20, collective_id=0, has_side_effects=True
        ),
    )(decoder, neighbours, area, tokens, weight, observed, output_weight)


def finish_kernel(
    output_scale, decoder_scale, middle, joint, rows, decoder, decoder_sum,
    cotangent_far, output_far, decoder_far, cotangent, output, decoder_near, sems,
):
    copies = []

    def send(near, far, part):
        copy = pltpu.make_async_copy(near.at[part], far.at[part], sems.at[len(copies)])
        copy.start()
        copies.append(copy)

    cores, spots, chunk, _ = decoder_sum.shape
    for spot in range(spots):
        for core in range(cores):
            at = (cores * spot + core) * chunk
            decoder_near[at : at + chunk, :] = decoder_sum[core, spot].astype(f32) * decoder_scale
    send(decoder_near, decoder_far, slice(None))
    output[...] = score(rows[...].reshape(output.shape[0], -1), decoder[...]) * output_scale
    send(output, output_far, slice(None))
    size = cotangent.shape[0] // 2
    for part in range(2):
        at = slice(part * size, (part + 1) * size)
        cotangent[at, :] = score(middle[at, :], joint[...]).astype(bf16)
        send(cotangent, cotangent_far, pl.ds(part * size, size))
    for copy in copies:
        copy.wait()


def finish(middle, joint, rows, decoder, decoder_sum, output_scale, decoder_scale):
    width, fields = decoder.shape
    shapes = [
        jax.ShapeDtypeStruct((middle.shape[0], width), bf16),
        jax.ShapeDtypeStruct((rows.shape[0] * rows.shape[1], width), f32),
        jax.ShapeDtypeStruct((width, fields), f32),
    ]
    return pl.pallas_call(
        functools.partial(finish_kernel, output_scale, decoder_scale),
        in_specs=[pl.BlockSpec(memory_space=pltpu.VMEM)] * 5,
        out_specs=[pl.BlockSpec(memory_space=pl.ANY)] * 3,
        out_shape=shapes,
        scratch_shapes=[pltpu.VMEM(shape.shape, shape.dtype) for shape in shapes]
        + [pltpu.SemaphoreType.DMA((4,))],
        compiler_params=pltpu.CompilerParams(vmem_limit_bytes=16 << 20),
    )(middle, joint, rows, decoder, decoder_sum)


def body(tokens, input_weight, output_weight, decoder_weight, neighbours, observed, cell_area):
    own_tokens = tokens[0]
    tok_rows, width = own_tokens.shape
    fields = decoder_weight.shape[1]
    seqs = lax.axis_size("seq")
    members = lax.axis_size("member")
    grid_rows = neighbours.shape[0]
    middle, rows, decoder_sum, joint = layer(
        decoder_weight, neighbours.T, cell_area[None, :], own_tokens, input_weight, observed,
        output_weight, seqs, members,
    )
    attention_cotangent, output_gradient, decoder_gradient = finish(
        middle, joint, rows, decoder_weight, decoder_sum,
        1.0 / math.sqrt(members * tok_rows * seqs), 1.0 / math.sqrt(members * grid_rows * seqs),
    )
    return (attention_cotangent[None], output_gradient, decoder_gradient)


def solution(mesh):
    in_specs = (
        P(("group", "member"), "seq", None),
        P(),
        P(),
        P(),
        P("seq", None),
        P(("group", "seq"), None),
        P("seq"),
    )
    out_specs = (P(("group", "member"), "seq", None), P(("group", "seq"), None), P("group", None))
    return jax.shard_map(body, mesh=mesh, in_specs=in_specs, out_specs=out_specs, check_vma=False)
```

```python
import functools
import math

import jax
import jax.numpy as jnp
from jax import lax
from jax.experimental import pallas as pl
from jax.experimental.pallas import tpu as pltpu
from jax.sharding import PartitionSpec as P

HEAD_DIM = 64
WINDOW = 512
REACH = 128
LANES = 128
COLS = 512

smooth = 0.1
f32 = jnp.float32
bf16 = jnp.bfloat16


def normalize(rows):
    values = rows.astype(f32)
    centre = jnp.mean(values, axis=-1, keepdims=True)
    values = values - centre
    spread = jnp.mean(values * values, axis=-1, keepdims=True)
    return (values * lax.rsqrt(spread + 1e-05)).astype(bf16)


def place_columns(mixed, scale):
    side = 256
    down = lax.broadcasted_iota(jnp.int32, (side, side), 0) >> 6
    across = lax.broadcasted_iota(jnp.int32, (side, side), 1) >> 6
    same = jnp.where(down == across, 1.0 / HEAD_DIM, 0.0).astype(bf16)
    pieces = []
    for at in range(0, mixed.shape[1], side):
        piece = mixed[:, at : at + side]
        mean = jnp.dot((piece * piece).astype(bf16), same, preferred_element_type=f32)
        pieces.append((piece * (lax.rsqrt(mean + 1e-06) * scale)).astype(bf16))
    return jnp.concatenate(pieces, axis=1)


def project(normed, weight, out, first, waits):
    width = weight.shape[0]
    for at in range(first, weight.shape[1], COLS):
        if waits:
            waits[at // COLS].wait()
        mixed = jnp.dot(normed[...], weight[:, at : at + COLS], preferred_element_type=f32)
        if at < 2 * width:
            mixed = place_columns(mixed, HEAD_DIM**-0.5 if at < width else 1.0)
        out[:, at - first : at - first + COLS] = mixed.astype(bf16)


def lane_block(j):
    return pl.ds(pl.multiple_of(j * LANES, LANES), LANES)


def low_lanes():
    return lax.broadcasted_iota(jnp.int32, (1, LANES), 1) < HEAD_DIM


def one_head(pair, head):
    return jnp.where(low_lanes() == (head == 0), pair, jnp.zeros_like(pair))


def with_counts(pair, head, real):
    ones = jnp.full(pair.shape, real, f32).astype(bf16)
    first = low_lanes()
    return jnp.where(first, pair, ones) if head == 0 else jnp.where(first, ones, pair)


def score(query, keys):
    return lax.dot_general(query, keys, (((1,), (1,)), ((), ())), preferred_element_type=f32)


def window_corner(scores, upper):
    rows = scores.shape[0] // 2
    down = lax.broadcasted_iota(jnp.int32, (rows, rows), 0)
    across = lax.broadcasted_iota(jnp.int32, (rows, rows), 1)
    late = across >= down
    blank = jnp.zeros((rows, rows), bf16)

    def corner(piece):
        weights = jnp.exp(piece)
        return (jnp.where(late, weights, 0.0) if upper else jnp.where(late, 0.0, weights)).astype(bf16)

    ends = (corner(scores[:rows, :rows]), corner(scores[rows:, rows:]))
    if upper:
        rest = jnp.exp(scores[:rows, rows:]).astype(bf16)
        lines = [[ends[0], rest], [blank, ends[1]]]
    else:
        rest = jnp.exp(scores[rows:, :rows]).astype(bf16)
        lines = [[ends[0], blank], [rest, ends[1]]]
    return jnp.concatenate([jnp.concatenate(line, axis=1) for line in lines], axis=0)


def attend_own(j, own, partial):
    rows, width = own.shape[0], own.shape[1] // 3
    half = rows // 2
    query = own[:, lane_block(j)]
    keys = own[:, lane_block(j + width // LANES)]
    values = own[:, lane_block(j + 2 * (width // LANES))]
    for head in range(2):
        scores = score(one_head(query, head), keys)
        early = [
            jnp.exp(scores[:half, :half]).astype(bf16), window_corner(scores[:half, half:], False),
        ]
        later = [
            window_corner(scores[half:, :half], True), jnp.exp(scores[half:, half:]).astype(bf16),
        ]
        weights = jnp.concatenate(
            [jnp.concatenate(early, axis=1), jnp.concatenate(later, axis=1)], axis=0
        )
        partial[2 * j + head] = jnp.dot(
            weights, with_counts(values, head, 1.0), preferred_element_type=f32
        )


def attend_beside(j, index, own, side, partial, attended, there):
    width = attended.shape[1]
    half = own.shape[0] // 2
    rows = slice(index * half, (index + 1) * half)
    query = own[rows, lane_block(j)]
    keys = side[rows, lane_block(j)]
    values = side[rows, lane_block(j + width // LANES)]
    totals = []
    for head in range(2):
        weights = window_corner(score(one_head(query, head), keys), index == 0)
        totals.append(
            jnp.dot(weights, with_counts(values, head, there), preferred_element_type=f32)
            + partial[2 * j + head, rows, :]
        )
    first = low_lanes()
    above = jnp.where(first, totals[0], totals[1])
    below = jnp.where(
        first, pltpu.roll(totals[0], HEAD_DIM, 1), pltpu.roll(totals[1], HEAD_DIM, 1)
    )
    attended[rows, lane_block(j)] = (above / below).astype(bf16)


def slope(diff):
    return diff * lax.rsqrt(diff * diff + smooth * smooth)


def copy_to(source, target, send, arrive, seq, member):
    return pltpu.make_async_remote_copy(
        src_ref=source,
        dst_ref=target,
        send_sem=send,
        recv_sem=arrive,
        device_id={"seq": seq, "member": member},
        device_id_type=pl.DeviceIdType.MESH,
    )


def layer_kernel(
    seqs, members, decoder, neighbours, area, tokens_far, weight_far, observed_far, output_far,
    middle_out, rows_out, decoder_out, joint,
    every, counts, turned, middle, edges, edges_in, terms, terms_in, pair, pair_in,
    sums, sums_in, mine,
    gathered_rows, gathered, tokens, attended, observed, output_weight,
    weight, normed, beside, own_parts, side_parts, mapped, partial, seen,
    attended_turned, latent_turned, rims, rims_in, pooled,
    halo_send, halo_in, met,
    local_sem, rim_send, rim_in, field_send, field_in, side_send, side_in, edge_send, edge_in, core_send, core_in,
    term_send, term_in,
    sum_send, sum_in, row_send, row_in, all_send, all_in,
):
    s, m = lax.axis_index("seq"), lax.axis_index("member")
    peers = seqs * members
    ranks, x, c = members // 2, m // 2, lax.rem(m, 2)
    sibling = m + 1 - 2 * c
    tok_rows, fields = mapped.shape
    fan, grid_rows = neighbours.shape
    wide = tok_rows + 2 * REACH
    width = tokens.shape[1]
    chunk = width // peers

    barrier = pltpu.get_barrier_semaphore()

    def tell(semaphore, seq, member):
        pl.semaphore_signal(
            semaphore, inc=1, device_id={"seq": seq, "member": member},
            device_id_type=pl.DeviceIdType.MESH,
        )

    has_left, has_right = s > 0, s < seqs - 1

    @pl.when(has_left)
    def _():
        tell(barrier, s - 1, m)

    @pl.when(has_right)
    def _():
        tell(barrier, s + 1, m)

    for step in range(1, members):
        tell(barrier, s, lax.rem(m + step, members))

    columns = weight.shape[1] // COLS
    loads = [
        pltpu.make_async_copy(far, near, local_sem.at[i])
        for i, (far, near) in enumerate(
            [(tokens_far, tokens)]
            + [
                (weight_far.at[:, pl.ds(i * COLS, COLS)], weight.at[:, pl.ds(i * COLS, COLS)])
                for i in range(columns)
            ]
            + [(output_far, output_weight), (observed_far, observed)]
        )
    ]
    for load in loads:
        load.start()
    half = WINDOW // 2

    def halo_copy(to_right):
        start, land, seq = (tok_rows - half, 0, s + 1) if to_right else (0, half, s - 1)
        return copy_to(
            tokens_far.at[pl.ds(start, half), :], beside.at[pl.ds(land, half), :],
            halo_send.at[to_right], halo_in.at[to_right], seq, m,
        )

    @pl.when(jnp.logical_not(has_left))
    def _():
        beside[:half, :] = jnp.zeros((half, width), bf16)

    @pl.when(jnp.logical_not(has_right))
    def _():
        beside[half:, :] = jnp.zeros((half, width), bf16)

    near = members - 1 + jnp.minimum(s, 1) + jnp.minimum(seqs - 1 - s, 1)
    pl.semaphore_wait(barrier, near)

    @pl.when(has_right)
    def _():
        halo_copy(1).start()

    @pl.when(has_left)
    def _():
        halo_copy(0).start()

    loads[0].wait()
    normed[...] = normalize(tokens[...])
    project(normed, weight, own_parts, 0, loads[1 : 1 + columns])
    loads[1 + columns].wait()
    joint[...] = jnp.dot(
        output_weight[...], decoder[...], preferred_element_type=f32
    ).astype(bf16)
    mapped[...] = jnp.dot(tokens[...], decoder[...], preferred_element_type=f32)
    base = s * tok_rows - REACH
    block = 128
    loads[2 + columns].wait()

    @pl.loop(0, grid_rows // block)
    def _(i):
        cells = pl.ds(pl.multiple_of(i * block, block), block)
        local = neighbours[:, cells] - base
        place = lax.broadcasted_iota(jnp.int32, (wide, block), 0)
        total = jnp.zeros((wide, block), f32)
        for k in range(fan):
            total += jnp.where(local[k : k + 1, :] == place, 1.0 / fan, 0.0)
        counts[:, cells] = total.astype(bf16)
        seen[:, cells] = observed[cells, :].T

    blocks = width // LANES
    group = math.gcd(blocks, 4)

    @pl.loop(0, blocks // group)
    def _(i):
        for k in range(group):
            attend_own(i * group + k, own_parts, partial)

    @pl.when(has_left)
    def _():
        halo_copy(0).wait_send()
        halo_copy(1).wait_recv()

    @pl.when(has_right)
    def _():
        halo_copy(1).wait_send()
        halo_copy(0).wait_recv()

    def meet(round, receive):
        far = 2 << round

        @pl.when(s >= far)
        def _():
            if receive:
                pl.semaphore_wait(met.at[round, 0], 1)
            else:
                tell(met.at[round, 1], s - far, m)

        @pl.when(s + far < seqs)
        def _():
            if receive:
                pl.semaphore_wait(met.at[round, 1], 1)
            else:
                tell(met.at[round, 0], s + far, m)

    rounds = max(0, (seqs - 1).bit_length() - 1)
    if rounds:
        meet(0, False)
    normed[...] = normalize(beside[...])
    project(normed, weight, side_parts, width, None)
    bands = (
        (REACH, half), (REACH + half, half), (0, REACH), (REACH + tok_rows, REACH),
    )

    def field_copy(core, band, step):
        start, size = bands[band]
        cells = pl.ds(start, size)
        here = step if core else 0
        there = ranks * core + step
        member = sibling if core else 2 * lax.rem(x + step, ranks) + c
        return copy_to(
            every.at[pl.ds(here * fields, fields), cells],
            every.at[pl.ds(there * fields, fields), cells],
            field_send.at[band, there], field_in.at[band, there], s, member,
        )

    def side_copy(side):
        start, land, seq = ((tok_rows, 0, s + 1), (REACH, REACH + tok_rows, s - 1))[side]
        return copy_to(
            every.at[pl.ds(0, fields), pl.ds(start, REACH)],
            every.at[pl.ds(0, fields), pl.ds(land, REACH)],
            side_send.at[side], side_in.at[side], seq, m,
        )

    def rim_copy(side):
        return copy_to(
            rims.at[side], rims_in.at[1 - side], rim_send.at[side], rim_in.at[side],
            s - 1 if side == 0 else s + 1, m,
        )

    def share(band):
        for step in range(1, ranks):
            field_copy(0, band, step).start()
        field_copy(1, band, 0).start()

    def forward(band):
        for step in range(1, ranks):
            field_copy(0, band, step).wait_recv()
            field_copy(1, band, step).start()

    def settle(band):
        for step in range(1, ranks):
            field_copy(0, band, step).wait_send()
        for step in range(ranks):
            field_copy(1, band, step).wait()

    for index in range(2):
        there = jnp.where((has_left, has_right)[index], 1.0, 0.0).astype(f32)
        for j in range(blocks):
            attend_beside(j, index, own_parts, side_parts, partial, attended, there)
        at = index * half
        total = mapped[at : at + half, :] + jnp.dot(
            attended[at : at + half, :], joint[...], preferred_element_type=f32
        )
        every[:fields, REACH + at : REACH + at + half] = total.T.astype(bf16)
        share(index)

        @pl.when((has_left, has_right)[index])
        def _():
            side_copy(1 - index).start()

    @pl.when(jnp.logical_not(has_left))
    def _():
        every[:, :REACH] = jnp.zeros((members * fields, REACH), bf16)
        rims_in[0] = jnp.zeros((width, REACH), bf16)
        edges_in[0] = jnp.zeros((REACH, fields), bf16)

    @pl.when(jnp.logical_not(has_right))
    def _():
        every[:, wide - REACH :] = jnp.zeros((members * fields, REACH), bf16)
        rims_in[1] = jnp.zeros((width, REACH), bf16)
        edges_in[1] = jnp.zeros((REACH, fields), bf16)

    def settle_latent(index):
        rows = slice(index * half, (index + 1) * half)
        latent = tokens[rows, :].astype(f32) + jnp.dot(
            attended[rows, :], output_weight[...], preferred_element_type=f32
        )
        columns = latent.astype(bf16).T
        latent_turned[:, index * half : (index + 1) * half] = columns
        rims[index] = columns[:, half - REACH :] if index else columns[:, :REACH]

        @pl.when((has_left, has_right)[index])
        def _():
            rim_copy(index).start()

    settle_latent(0)

    @pl.when(has_right)
    def _():
        side_copy(1).wait_recv()
        share(3)

    forward(0)
    settle_latent(1)

    @pl.when(has_left)
    def _():
        side_copy(0).wait_recv()
        share(2)

    attended_turned[...] = attended[...].T
    forward(1)

    @pl.when(has_right)
    def _():
        forward(3)
        side_copy(0).wait_send()

    @pl.when(has_left)
    def _():
        forward(2)
        side_copy(1).wait_send()

    settle(0)
    settle(1)
    block = math.gcd(grid_rows, 256)
    cuts = [slice(at, at + block) for at in range(0, grid_rows, block)]
    for cells in cuts:
        pooled[:, cells] = jnp.dot(
            every[:, REACH : wide - REACH], counts[REACH : wide - REACH, cells],
            preferred_element_type=f32,
        )

    @pl.when(has_right)
    def _():
        settle(3)

    @pl.when(has_left)
    def _():
        settle(2)

    outer = jnp.concatenate([every[:, :REACH], every[:, wide - REACH :]], axis=1)
    for cells in cuts:
        places = jnp.concatenate([counts[:REACH, cells], counts[wide - REACH :, cells]], axis=0)
        found = pooled[:, cells] + jnp.dot(outer, places, preferred_element_type=f32)
        mean = found[:fields, :]
        pairs = jnp.zeros((fields, block), f32)
        for step in range(1, members):
            pairs += slope(mean - found[step * fields : (step + 1) * fields, :])
        single = slope(mean - seen[:, cells])
        turned[:, cells] = (
            area[:, cells]
            * (single * (1.0 / members) - pairs * (1.0 / (members * (members - 1))))
        ).astype(bf16)

    def spread(places):
        return score(places, turned[...])

    reached = spread(counts[...])
    rounded = reached.astype(bf16)
    edges[0] = rounded[:REACH]
    edges[1] = rounded[wide - REACH :]

    def edge_copy(side):
        return copy_to(
            edges.at[side], edges_in.at[1 - side], edge_send.at[side], edge_in.at[side],
            s - 1 if side == 0 else s + 1, m,
        )

    @pl.when(has_left)
    def _():
        edge_copy(0).start()

    @pl.when(has_right)
    def _():
        edge_copy(1).start()

    middle[...] = reached[REACH : wide - REACH]
    latent_term = jnp.dot(
        latent_turned[...], rounded[REACH : wide - REACH], preferred_element_type=f32
    )

    @pl.when(has_left)
    def _():
        rim_copy(0).wait_send()
        rim_copy(1).wait_recv()

    @pl.when(has_right)
    def _():
        rim_copy(1).wait_send()
        rim_copy(0).wait_recv()

    for round in range(rounds):
        meet(round, True)
        if round + 1 < rounds:
            meet(round + 1, False)

    spots = seqs * ranks
    spot = s * ranks + x

    def put(part, value):
        rows = value.astype(bf16)
        for core in range(2):
            for rank in range(ranks):
                for seq in range(seqs):
                    at = (seq * members + 2 * rank + core) * chunk
                    terms[part, core, rank, seq] = rows[at : at + chunk, :]

    def core_copy(part):
        return copy_to(
            terms.at[part, 1 - c], terms_in.at[part], core_send.at[part], core_in.at[part],
            s, sibling,
        )

    def rank_copy(part, step):
        rank = lax.rem(x + step, ranks)
        return copy_to(
            pair.at[part, rank], pair_in.at[part, step],
            term_send.at[part, step], term_in.at[part, step], s, 2 * rank + c,
        )

    def sum_copy(part, step):
        seq = lax.rem(s + step, seqs)
        return copy_to(
            sums.at[part, seq], sums_in.at[part, step],
            sum_send.at[part, step], sum_in.at[part, step], seq, m,
        )

    def row_copy(step):
        return copy_to(
            mine.at[0], gathered_rows.at[m], row_send.at[step], row_in.at[step],
            s, lax.rem(m + step, members),
        )

    def all_copy(step):
        other = lax.rem(spot + step, spots)
        return copy_to(
            mine.at[1], gathered.at[c, spot], all_send.at[step], all_in.at[step],
            other // ranks, 2 * lax.rem(other, ranks) + c,
        )

    def last_copy():
        return copy_to(
            gathered.at[c], gathered.at[c], core_send.at[2], core_in.at[2], s, sibling
        )

    def add_cores(part):
        core_copy(part).wait()
        pair[part] = (terms[part, c].astype(f32) + terms_in[part].astype(f32)).astype(bf16)
        for step in range(1, ranks):
            rank_copy(part, step).start()

    def add_ranks(part):
        for step in range(1, ranks):
            rank_copy(part, step).wait()
        total = pair[part, x].astype(f32)
        for step in range(1, ranks):
            total += pair_in[part, step].astype(f32)
        sums[part] = total.astype(bf16)

        for step in range(1, seqs):
            sum_copy(part, step).start()

    def add_seqs(part):
        for step in range(1, seqs):
            sum_copy(part, step).wait()

        total = sums[part, s].astype(f32)
        for step in range(1, seqs):
            total += sums_in[part, step].astype(f32)
        mine[part] = total.astype(bf16)

    put(1, latent_term + jnp.dot(
        jnp.concatenate([rims_in[0], rims_in[1]], axis=1),
        jnp.concatenate([rounded[:REACH], rounded[wide - REACH :]], axis=0),
        preferred_element_type=f32,
    ))
    core_copy(1).start()
    add_cores(1)

    @pl.when(has_left)
    def _():
        edge_copy(0).wait_send()
        edge_copy(1).wait_recv()

    @pl.when(has_right)
    def _():
        edge_copy(1).wait_send()
        edge_copy(0).wait_recv()

    middle[:REACH, :] += edges_in[0].astype(f32)
    middle[tok_rows - REACH :, :] += edges_in[1].astype(f32)
    whole = middle[...].astype(bf16)
    middle_out[...] = whole
    put(0, jnp.dot(attended_turned[...], whole, preferred_element_type=f32))
    core_copy(0).start()
    add_cores(0)
    add_ranks(1)
    add_ranks(0)
    add_seqs(1)

    for step in range(1, spots):
        all_copy(step).start()

    add_seqs(0)
    for step in range(1, members):
        row_copy(step).start()
    gathered_rows[m] = mine[0]
    gathered[c, spot] = mine[1]
    for step in range(1, members):
        row_copy(step).wait()
    rows_out[...] = gathered_rows[...]

    for step in range(1, spots):
        all_copy(step).wait()

    last_copy().start()
    last_copy().wait()
    decoder_out[...] = gathered[...]


def layer(decoder, neighbours, area, tokens, weight, observed, output_weight, seqs, members):
    tok_rows, width = tokens.shape
    fields = decoder.shape[1]
    grid_rows = neighbours.shape[1]
    wide = tok_rows + 2 * REACH
    ranks = members // 2
    chunk = width // (seqs * members)
    near = pl.BlockSpec(memory_space=pltpu.VMEM)
    far = pl.BlockSpec(memory_space=pl.ANY)
    dma = pltpu.SemaphoreType.DMA
    return pl.pallas_call(
        functools.partial(layer_kernel, seqs, members),
        in_specs=[near] * 3 + [far] * 4,
        out_specs=[near] * 4,
        out_shape=[
            pltpu.VMEM((tok_rows, fields), bf16),
            pltpu.VMEM((members, chunk, fields), bf16),
            pltpu.VMEM((2, seqs * ranks, chunk, fields), bf16),
            pltpu.VMEM((width, fields), bf16),
        ],
        scratch_shapes=[
            pltpu.VMEM((members * fields, wide), bf16),
            pltpu.VMEM((wide, grid_rows), bf16),
            pltpu.VMEM((fields, grid_rows), bf16),
            pltpu.VMEM((tok_rows, fields), f32),
            pltpu.VMEM((2, REACH, fields), bf16),
            pltpu.VMEM((2, REACH, fields), bf16),
            pltpu.VMEM((2, 2, ranks, seqs, chunk, fields), bf16),
            pltpu.VMEM((2, ranks, seqs, chunk, fields), bf16),
            pltpu.VMEM((2, ranks, seqs, chunk, fields), bf16),
            pltpu.VMEM((2, ranks, seqs, chunk, fields), bf16),
            pltpu.VMEM((2, seqs, chunk, fields), bf16),
            pltpu.VMEM((2, seqs, chunk, fields), bf16),
            pltpu.VMEM((2, chunk, fields), bf16),
            pltpu.VMEM((members, chunk, fields), bf16),
            pltpu.VMEM((2, seqs * ranks, chunk, fields), bf16),
            pltpu.VMEM(tokens.shape, bf16),
            pltpu.VMEM(tokens.shape, bf16),
            pltpu.VMEM(observed.shape, f32),
            pltpu.VMEM(output_weight.shape, bf16),
            pltpu.VMEM(weight.shape, bf16),
            pltpu.VMEM(tokens.shape, bf16),
            pltpu.VMEM((WINDOW, width), bf16),
            pltpu.VMEM((tok_rows, 3 * width), bf16),
            pltpu.VMEM((WINDOW, 2 * width), bf16),
            pltpu.VMEM((tok_rows, fields), f32),
            pltpu.VMEM((2 * (width // LANES), tok_rows, LANES), f32),
            pltpu.VMEM((fields, grid_rows), f32),
            pltpu.VMEM((width, tok_rows), bf16),
            pltpu.VMEM((width, tok_rows), bf16),
            pltpu.VMEM((2, width, REACH), bf16),
            pltpu.VMEM((2, width, REACH), bf16),
            pltpu.VMEM((members * fields, grid_rows), f32),
            dma((2,)),
            dma((2,)),
            pltpu.SemaphoreType.REGULAR((max(1, (seqs - 1).bit_length() - 1), 2)),
            dma((3 + weight.shape[1] // COLS,)),
            dma((2,)),
            dma((2,)),
            dma((4, members)),
            dma((4, members)),
            dma((2,)),
            dma((2,)),
            dma((2,)),
            dma((2,)),
            dma((3,)),
            dma((3,)),
            dma((2, ranks)),
            dma((2, ranks)),
            dma((2, seqs)),
            dma((2, seqs)),
            dma((members,)),
            dma((members,)),
            dma((seqs * ranks,)),
            dma((seqs * ranks,)),
        ],
        compiler_params=pltpu.CompilerParams(
            vmem_limit_bytes=56 << 20, collective_id=0, has_side_effects=True
        ),
    )(decoder, neighbours, area, tokens, weight, observed, output_weight)


def finish_kernel(
    output_scale, decoder_scale, middle, joint, rows, decoder, decoder_sum,
    cotangent_far, output_far, decoder_far, cotangent, output, decoder_near, sems,
):
    copies = []

    def send(near, far, part):
        copy = pltpu.make_async_copy(near.at[part], far.at[part], sems.at[len(copies)])
        copy.start()
        copies.append(copy)

    cores, spots, chunk, _ = decoder_sum.shape
    for spot in range(spots):
        for core in range(cores):
            at = (cores * spot + core) * chunk
            decoder_near[at : at + chunk, :] = decoder_sum[core, spot].astype(f32) * decoder_scale
    send(decoder_near, decoder_far, slice(None))
    output[...] = score(rows[...].reshape(output.shape[0], -1), decoder[...]) * output_scale
    send(output, output_far, slice(None))
    size = cotangent.shape[0] // 2
    for part in range(2):
        at = slice(part * size, (part + 1) * size)
        cotangent[at, :] = score(middle[at, :], joint[...]).astype(bf16)
        send(cotangent, cotangent_far, pl.ds(part * size, size))
    for copy in copies:
        copy.wait()


def finish(middle, joint, rows, decoder, decoder_sum, output_scale, decoder_scale):
    width, fields = decoder.shape
    shapes = [
        jax.ShapeDtypeStruct((middle.shape[0], width), bf16),
        jax.ShapeDtypeStruct((rows.shape[0] * rows.shape[1], width), f32),
        jax.ShapeDtypeStruct((width, fields), f32),
    ]
    return pl.pallas_call(
        functools.partial(finish_kernel, output_scale, decoder_scale),
        in_specs=[pl.BlockSpec(memory_space=pltpu.VMEM)] * 5,
        out_specs=[pl.BlockSpec(memory_space=pl.ANY)] * 3,
        out_shape=shapes,
        scratch_shapes=[pltpu.VMEM(shape.shape, shape.dtype) for shape in shapes]
        + [pltpu.SemaphoreType.DMA((4,))],
        compiler_params=pltpu.CompilerParams(vmem_limit_bytes=16 << 20),
    )(middle, joint, rows, decoder, decoder_sum)


def body(tokens, input_weight, output_weight, decoder_weight, neighbours, observed, cell_area):
    own_tokens = tokens[0]
    tok_rows, width = own_tokens.shape
    fields = decoder_weight.shape[1]
    seqs = lax.axis_size("seq")
    members = lax.axis_size("member")
    grid_rows = neighbours.shape[0]
    middle, rows, decoder_sum, joint = layer(
        decoder_weight, neighbours.T, cell_area[None, :], own_tokens, input_weight, observed,
        output_weight, seqs, members,
    )
    attention_cotangent, output_gradient, decoder_gradient = finish(
        middle, joint, rows, decoder_weight, decoder_sum,
        1.0 / math.sqrt(members * tok_rows * seqs), 1.0 / math.sqrt(members * grid_rows * seqs),
    )
    return (attention_cotangent[None], output_gradient, decoder_gradient)


def solution(mesh):
    in_specs = (
        P(("group", "member"), "seq", None),
        P(),
        P(),
        P(),
        P("seq", None),
        P(("group", "seq"), None),
        P("seq"),
    )
    out_specs = (P(("group", "member"), "seq", None), P(("group", "seq"), None), P("group", None))
    return jax.shard_map(body, mesh=mesh, in_specs=in_specs, out_specs=out_specs, check_vma=False)
```
